32 devices in a mesh: snap: 8 (over z, core), space: 4 (over y, x).
Axes of the slice: x: 2, y: 2, z: 4, core: 2. Of those that a mesh axis runs over, the one named last changes fastest.
Arguments:
- snapshots: bfloat16 [16384, 1024], P('space', 'snap'), may hold values from -36 to 36
Outputs:
- gram_band: float32 [1024, 640], P(('snap', 'space'))
- mean_field: float32 [16384], P('space')
The draws below stay inside these ranges and needn't reach their ends.
All inputs are finite; a program needn't handle non-finite values.
Results may differ from the reference program's by a relative error of at most 0.00036.
Values may be sent and summed in bfloat16 or wider, within the bound.
No kernel may reach another device: no remote copies, remote signals or barrier semaphores. Data moves between devices by JAX's collectives and lax.ppermute only.
A program may use at most 64 MiB of HBM per device.

```python
import jax
import jax.numpy as jnp
from jax import lax

SNAP_DEV = 128
ROWS = 16384
SNAPS = 1024
N_SNAP = 8


def draw_snapshots(key, part):
    key_level, key_scale, key_noise = jax.random.split(jax.random.fold_in(key, 17), 3)
    level = jnp.clip(jax.random.normal(key_level, (ROWS, 1), jnp.float32), -4.0, 4.0)
    moments = jnp.arange(SNAPS, dtype=jnp.float32)[None, :] / SNAPS
    ramp_values = 0.5 + moments
    row_scale = jnp.exp(jax.random.uniform(key_scale, (ROWS, 1), jnp.float32, jnp.log(0.3), jnp.log(3.0)))
    noise_values = jnp.clip(jax.random.normal(key_noise, (ROWS, SNAPS), jnp.float32), -4.0, 4.0)
    values = row_scale * (level * ramp_values + ramp_values * noise_values)
    return values.astype(jnp.bfloat16)


def setup_inputs(seed: int = 0) -> dict:
    key_list = jax.random.split(jax.random.key(seed), 2)
    snapshots = draw_snapshots(jax.random.fold_in(key_list[1], 71), 0)
    return dict(snapshots=snapshots)


def reference(snapshots):
    mean_field = jnp.sum(snapshots.astype(jnp.float32), axis=1) / SNAPS
    fluctuation = (snapshots.astype(jnp.float32) - mean_field[:, None]).astype(jnp.bfloat16)
    band_blocks = N_SNAP // 2 + 1
    extended = jnp.concatenate([fluctuation, fluctuation[:, :band_blocks * SNAP_DEV]], axis=1)

    def one_row(block_index):
        first_col = (block_index * SNAP_DEV).astype(jnp.int32)
        own_block = lax.dynamic_slice_in_dim(fluctuation, first_col, SNAP_DEV, 1)
        window = lax.dynamic_slice_in_dim(extended, first_col, band_blocks * SNAP_DEV, 1)
        return jnp.dot(own_block.T, window, preferred_element_type=jnp.float32)

    rows_out = lax.map(one_row, jnp.arange(N_SNAP, dtype=jnp.int32))
    gram_band = rows_out.reshape(SNAPS, band_blocks * SNAP_DEV) * (1.0 / ROWS)
    return gram_band, mean_field
```

```python
import functools

import jax
import jax.numpy as jnp
from jax import lax
from jax.experimental import pallas as pl
from jax.experimental.pallas import tpu as pltpu
from jax.sharding import PartitionSpec as P

ROW_TILE = 128


def bits_of(count):
    return [1 << n for n in range(count.bit_length() - 1)]


def part_position(part, space, core, space_count):
    bits = bits_of(space_count)
    position = 0
    for step in range(len(bits)):
        other = bits[(step + 1) % len(bits)]
        bit = jnp.where(core == 0, bits[step], other)
        position = position * 2 + jnp.where(((part ^ space) & bit) != 0, 1, 0)
    return position


def hub_kernel(sizes, place_ref, *refs):
    snap_count, space_count, chunk, width, total_columns = sizes
    blocks, (out_ref, fluct) = refs[:-2], refs[-2:]
    me, space = place_ref[0], place_ref[1]
    core = me % 2
    band = snap_count // 2 + 1
    part_rows = width // space_count

    def subtract(half, source_of, tile):
        rows = pl.ds(pl.multiple_of(tile * ROW_TILE, ROW_TILE), ROW_TILE)
        held = []
        for offset in range(snap_count):
            ref, base = source_of(offset)
            picked = pl.ds(pl.multiple_of(base + tile * ROW_TILE, ROW_TILE), ROW_TILE)
            held.append(ref[picked, :].astype(jnp.float32))
        whole = functools.reduce(jnp.add, held)
        mean = jnp.sum(whole, axis=1, keepdims=True) * (1.0 / total_columns)
        target = pl.ds(pl.multiple_of(half * chunk + tile * ROW_TILE, ROW_TILE), ROW_TILE)
        del rows
        owner = me if half == 0 else me ^ 1
        for offset in range(snap_count):
            slot = owner ^ offset
            value = (held[offset] - mean).astype(jnp.bfloat16)
            fluct[target, pl.ds(pl.multiple_of(slot * width, width), width)] = value

            @pl.when(slot < band - 1)
            def _():
                fluct[target, pl.ds(pl.multiple_of((slot + snap_count) * width, width), width)] = value

    own_ref, mate_ref = blocks[0], blocks[1]
    mine = lambda offset: (
        (own_ref, core * chunk) if offset == 0 else (mate_ref, core * chunk) if offset == 1 else (blocks[offset], 0)
    )
    theirs = lambda offset: (
        (mate_ref, (1 - core) * chunk)
        if offset == 0
        else (own_ref, (1 - core) * chunk)
        if offset == 1
        else (blocks[snap_count - 2 + offset], 0)
    )
    for half, source_of in ((0, mine), (1, theirs)):

        def one_tile(tile, carry, half=half, source_of=source_of):
            subtract(half, source_of, tile)
            return carry

        lax.fori_loop(0, chunk // ROW_TILE, one_tile, 0)

    def one_block(rel, carry):
        block = ((me // 2) ^ rel) * 2 + core
        first = pl.multiple_of(block * width, width)
        left = fluct[:, pl.ds(first, width)]
        window = fluct[:, pl.ds(first, band * width)]
        tiles = lax.dot_general(left, window, (((0,), (0,)), ((), ())), preferred_element_type=jnp.float32)
        for part in range(space_count):
            position = part_position(part, space, core, space_count)
            out_ref[position, rel] = tiles[part * part_rows : (part + 1) * part_rows, :]
        return carry

    lax.fori_loop(0, snap_count // 2, one_block, 0)


def per_device(snapshots):
    snap_count = lax.axis_size("snap")
    space_count = lax.axis_size("space")
    row_count, width = snapshots.shape
    me, space = lax.axis_index("snap"), lax.axis_index("space")
    core = me % 2
    hub_count = snap_count // 2
    first_hub = snap_count // 4
    hubs = list(range(first_hub, first_hub + hub_count))
    chunk = row_count // hub_count
    band = snap_count // 2 + 1
    part_rows = width // space_count

    def chip_rows(device):
        hub_chip = jnp.clip(device // 2 - first_hub // 2, 0, hub_count // 2 - 1)
        return lax.dynamic_slice_in_dim(snapshots, hub_chip * 2 * chunk, 2 * chunk, 0)

    def chunk_of(device):
        hub = jnp.clip(device - first_hub, 0, hub_count - 1)
        return lax.dynamic_slice_in_dim(snapshots, hub * chunk, chunk, 0)

    own = chip_rows(me)
    mate = lax.ppermute(own, "snap", [(h ^ 1, h) for h in hubs])
    order = sorted(range(2, snap_count), key=lambda t: (-(t.bit_length() == snap_count.bit_length() - 1 and t >= 3 * snap_count // 4), t))
    received = {t: lax.ppermute(chunk_of(me ^ t), "snap", [(h ^ t, h) for h in hubs]) for t in order}

    totals = jnp.sum(snapshots.astype(jnp.float32), axis=1)
    for bit in bits_of(snap_count):
        totals = totals + lax.ppermute(totals, "snap", [(i, i ^ bit) for i in range(snap_count)])
    mean_field = totals * (1.0 / (width * snap_count))

    passed = {t: lax.ppermute(received[t], "snap", [(h ^ 1, h) for h in hubs]) for t in order}

    place = jnp.stack([me, space]).astype(jnp.int32)
    vmem = pl.BlockSpec(memory_space=pltpu.VMEM)
    operands = [own, mate] + [received[t] for t in range(2, snap_count)] + [passed[t] for t in range(2, snap_count)]
    flops = 2 * hub_count * width * band * width * 2 * chunk
    partial = pl.pallas_call(
        functools.partial(hub_kernel, (snap_count, space_count, chunk, width, width * snap_count)),
        out_shape=jax.ShapeDtypeStruct((space_count, hub_count, part_rows, band * width), jnp.float32),
        in_specs=[pl.BlockSpec(memory_space=pltpu.SMEM)] + [vmem] * len(operands),
        out_specs=vmem,
        scratch_shapes=[pltpu.VMEM((2 * chunk, (snap_count + band - 1) * width), jnp.bfloat16)],
        cost_estimate=pl.CostEstimate(flops=flops, bytes_accessed=4 * chunk * snap_count * width, transcendentals=0),
        name="hub_gram",
    )(place, *operands)

    bits = bits_of(space_count)
    for step in range(len(bits)):
        half = partial.shape[0] // 2
        pairs = []
        for h in hubs:
            bit = bits[(step + h % 2) % len(bits)]
            pairs += [(h * space_count + s, h * space_count + (s ^ bit)) for s in range(space_count)]
        partial = partial[:half] + lax.ppermute(partial[half:], ("snap", "space"), pairs)

    summed = partial[0]
    is_hub = (me >= first_hub) & (me < first_hub + hub_count)
    gram_band = jnp.where(is_hub, summed[0], 0.0)
    for rel in range(1, hub_count):
        gram_band = gram_band + lax.ppermute(summed[rel], "snap", [(h, h ^ (2 * rel)) for h in hubs])
    return gram_band * (1.0 / (row_count * space_count)), mean_field


def solution(mesh):
    return jax.shard_map(
        per_device,
        mesh=mesh,
        in_specs=(P("space", "snap"),),
        out_specs=(P(("snap", "space"), None), P("space")),
        check_vma=False,
    )
```

```python
import functools

import jax
import jax.numpy as jnp
import numpy as np
from jax import lax
from jax.experimental import pallas as pl
from jax.experimental.pallas import tpu as pltpu
from jax.sharding import PartitionSpec as P


LANES = 128


def bits_of(count):
    return [1 << n for n in range(count.bit_length() - 1)]


def part_masks(space_count, core):
    bits = bits_of(space_count)
    taken = [bits[(step + core) % len(bits)] for step in range(len(bits))]
    masks = []
    for position in range(space_count):
        mask = 0
        for step, bit in enumerate(taken):
            if position >> (len(bits) - 1 - step) & 1:
                mask |= bit
        masks.append(mask)
    return masks


def tile_tables(snap_count, late):
    early_rows, late_rows = [], []
    for me in range(snap_count):
        parts = ([], [])
        for offset in range(snap_count // 2):
            block = ((me // 2) ^ offset) * 2 + me % 2
            for k in range(snap_count // 2 + 1):
                other = (((block + k) % snap_count) ^ me) // 2
                parts[int(late in (offset, other))].append((offset, k))
        early_rows.append(parts[0])
        late_rows.append(parts[1])

    def even(rows):
        longest = max(len(row) for row in rows)
        return np.array([row + [row[-1]] * (longest - len(row)) for row in rows], np.int32)

    return even(early_rows), even(late_rows)


def place_tiles(sizes, place_ref, table_ref, tiles_ref, keep_ref, send_ref):
    space_count, part_rows = sizes
    space, core = place_ref[1], place_ref[0] % 2
    masks = [part_masks(space_count, c) for c in (0, 1)]
    half = space_count // 2

    def one(slot, carry):
        offset, k = table_ref[0, slot], table_ref[1, slot]
        lanes = pl.ds(pl.multiple_of(k * LANES, LANES), LANES)
        for position in range(space_count):
            part = space ^ jnp.where(core == 0, masks[0][position], masks[1][position])
            rows = pl.ds(pl.multiple_of(part * part_rows, part_rows), part_rows)
            target = keep_ref if position < half else send_ref
            target[position % half, slot] = tiles_ref[offset, rows, lanes]
        return carry

    lax.fori_loop(0, table_ref.shape[1], one, 0)


def fluctuations(totals_ref, first_row, total_columns, tile):
    row = pl.ds(first_row // LANES + tile, 1)
    mean = totals_ref[row, :] * (1.0 / total_columns)
    return jnp.transpose(jnp.broadcast_to(mean, (LANES, LANES)))


def early_kernel(sizes, early, place_ref, table_ref, totals_ref, *refs):
    snap_count, space_count, rows, width = sizes
    blocks = refs[: 2 * len(early)]
    fluct_ref, keep_ref, send_ref, tiles_ref = refs[2 * len(early) :]
    me = place_ref[0]
    first_row = place_ref[2]
    band = snap_count // 2 + 1

    def one_tile(tile, carry):
        mean = fluctuations(totals_ref, first_row, width * snap_count, tile)
        target = pl.ds(pl.multiple_of(tile * LANES, LANES), LANES)
        for n, offset in enumerate(early):
            for other in (0, 1):
                ref = blocks[2 * n + other]
                base = first_row if offset == 0 else 0
                source = pl.ds(pl.multiple_of(base + tile * LANES, LANES), LANES)
                value = (ref[source, :].astype(jnp.float32) - mean).astype(jnp.bfloat16)
                slot = me ^ (2 * offset + other)
                fluct_ref[target, pl.ds(pl.multiple_of(slot * width, width), width)] = value

                @pl.when(slot < band - 1)
                def _():
                    again = pl.multiple_of((slot + snap_count) * width, width)
                    fluct_ref[target, pl.ds(again, width)] = value

        return carry

    lax.fori_loop(0, rows // LANES, one_tile, 0)
    for offset in early:
        block = ((me // 2) ^ offset) * 2 + me % 2
        first = pl.multiple_of(block * width, width)
        tiles_ref[offset] = lax.dot_general(
            fluct_ref[:, pl.ds(first, width)],
            fluct_ref[:, pl.ds(first, band * width)],
            (((0,), (0,)), ((), ())),
            preferred_element_type=jnp.float32,
        )
    place_tiles((space_count, width // space_count), place_ref, table_ref, tiles_ref, keep_ref, send_ref)


def late_kernel(sizes, late, place_ref, table_ref, totals_ref, same_ref, other_ref, early_ref, *refs):
    snap_count, space_count, rows, width = sizes
    keep_ref, send_ref, fluct_ref, tiles_ref = refs
    me = place_ref[0]
    first_row = place_ref[2]
    band = snap_count // 2 + 1
    core = me % 2

    def one_tile(tile, carry):
        mean = fluctuations(totals_ref, first_row, width * snap_count, tile)
        target = pl.ds(pl.multiple_of(tile * LANES, LANES), LANES)
        for ref, column in ((same_ref, core), (other_ref, 1 - core)):
            value = (ref[target, :].astype(jnp.float32) - mean).astype(jnp.bfloat16)
            fluct_ref[target, pl.ds(pl.multiple_of(column * width, width), width)] = value
        return carry

    lax.fori_loop(0, rows // LANES, one_tile, 0)

    def product(left, right):
        return lax.dot_general(left, right, (((0,), (0,)), ((), ())), preferred_element_type=jnp.float32)

    late_first = ((me // 2) ^ late) * 2
    for offset in range(snap_count // 2):
        block = ((me // 2) ^ offset) * 2 + core
        first = pl.multiple_of(block * width, width)
        if offset == late:
            left = fluct_ref[:, pl.ds(pl.multiple_of(core * width, width), width)]
            tiles_ref[offset] = product(left, early_ref[:, pl.ds(first, band * width)])
        else:
            left = early_ref[:, pl.ds(first, width)]
        pair = product(left, fluct_ref[...])
        for n in (0, 1):
            k = (late_first + n - block + snap_count) % snap_count

            @pl.when(k < band)
            def _():
                lanes = pl.ds(pl.multiple_of(k * width, width), width)
                tiles_ref[offset, :, lanes] = pair[:, n * width : (n + 1) * width]

    place_tiles((space_count, width // space_count), place_ref, table_ref, tiles_ref, keep_ref, send_ref)


def joined_kernel(width, early_table, late_table, *refs):
    first_keep, first_recv, second_keep, second_recv, out_ref = refs
    for table, keep, recv in ((early_table, first_keep, first_recv), (late_table, second_keep, second_recv)):

        def one(slot, carry, table=table, keep=keep, recv=recv):
            offset, k = table[0, slot], table[1, slot]
            lanes = pl.ds(pl.multiple_of(k * width, width), width)
            out_ref[offset, :, lanes] = keep[0, slot] + recv[0, slot]
            return carry

        lax.fori_loop(0, table.shape[1], one, 0)


def per_device(snapshots):
    snap_count = lax.axis_size("snap")
    space_count = lax.axis_size("space")
    row_count, width = snapshots.shape
    me, space = lax.axis_index("snap"), lax.axis_index("space")
    chip_count = snap_count // 2
    first_chip, hub_chips = chip_count // 4, chip_count // 2
    hubs = list(range(2 * first_chip, 2 * (first_chip + hub_chips)))
    rows = row_count // hub_chips
    band = chip_count + 1
    part_rows = width // space_count
    late = chip_count // 2
    early = [offset for offset in range(chip_count) if offset != late]

    def hub_rows(device):
        return jnp.clip(device // 2 - first_chip, 0, hub_chips - 1) * rows

    def to_hubs(offset):
        piece = lax.dynamic_slice_in_dim(snapshots, hub_rows(me ^ (2 * offset)), rows, 0)
        return lax.ppermute(piece, "snap", [(h ^ (2 * offset), h) for h in hubs])

    def to_other_core(x):
        return lax.ppermute(x, "snap", [(h, h ^ 1) for h in hubs])

    received = {offset: to_hubs(offset) for offset in early[1:] + [late]}
    mate = lax.ppermute(snapshots, "snap", [(i, i ^ 1) for i in range(snap_count)])

    totals = jnp.sum(snapshots.astype(jnp.float32), axis=1)
    for bit in bits_of(snap_count):
        there = lax.ppermute(totals, "snap", [(i, i ^ bit) for i in range(snap_count)])
        totals = totals + there
    mean_field = totals * (1.0 / (width * snap_count))
    lane_totals = totals.reshape(row_count // LANES, LANES)

    passed = {offset: to_other_core(received[offset]) for offset in received}

    place = jnp.stack([me, space, hub_rows(me)]).astype(jnp.int32)
    early_all, late_all = tile_tables(snap_count, late)
    early_table = lax.dynamic_index_in_dim(jnp.asarray(early_all.transpose(0, 2, 1)), me, 0, False)
    late_table = lax.dynamic_index_in_dim(jnp.asarray(late_all.transpose(0, 2, 1)), me, 0, False)
    smem = pl.BlockSpec(memory_space=pltpu.SMEM)
    vmem = pl.BlockSpec(memory_space=pltpu.VMEM)
    sizes = (snap_count, space_count, rows, width)
    columns = (snap_count + band - 1) * width
    product = 2 * width * width * rows

    def halves(slots):
        shape = jax.ShapeDtypeStruct((space_count // 2, slots, part_rows, width), jnp.float32)
        return [shape, shape]

    def grant(*shapes):
        total = sum(int(np.prod(s.shape)) * jnp.dtype(s.dtype).itemsize for s in shapes)
        return total + (8 << 20)

    tiles = jax.ShapeDtypeStruct((chip_count, width, band * width), jnp.float32)
    operands = [snapshots, mate]
    for offset in early[1:]:
        operands += [received[offset], passed[offset]]
    early_out = [jax.ShapeDtypeStruct((rows, columns), jnp.bfloat16)] + halves(early_all.shape[1])
    fluct, first_keep, first_send = pl.pallas_call(
        functools.partial(early_kernel, sizes, early),
        out_shape=early_out,
        in_specs=[smem, smem, vmem] + [vmem] * len(operands),
        out_specs=[vmem] * 3,
        scratch_shapes=[pltpu.VMEM(tiles.shape, jnp.float32)],
        cost_estimate=pl.CostEstimate(flops=product * len(early) * band, bytes_accessed=0, transcendentals=0),
        compiler_params=pltpu.CompilerParams(vmem_limit_bytes=grant(tiles, *operands, *early_out)),
        name="early_tiles",
    )(place, early_table, lane_totals, *operands)

    operands = [received[late], passed[late], fluct]
    late_out = halves(late_all.shape[1])
    late_fluct = jax.ShapeDtypeStruct((rows, 2 * width), jnp.bfloat16)
    second_keep, second_send = pl.pallas_call(
        functools.partial(late_kernel, sizes, late),
        out_shape=late_out,
        in_specs=[smem, smem, vmem] + [vmem] * len(operands),
        out_specs=[vmem] * 2,
        scratch_shapes=[pltpu.VMEM(late_fluct.shape, jnp.bfloat16), pltpu.VMEM(tiles.shape, jnp.float32)],
        cost_estimate=pl.CostEstimate(flops=product * (band + snap_count), bytes_accessed=0, transcendentals=0),
        compiler_params=pltpu.CompilerParams(vmem_limit_bytes=grant(tiles, late_fluct, *operands, *late_out)),
        name="late_tiles",
    )(place, late_table, lane_totals, *operands)

    bits = bits_of(space_count)

    def exchanged(x, step):
        pairs = []
        for h in hubs:
            bit = bits[(step + h % 2) % len(bits)]
            pairs += [(h * space_count + s, h * space_count + (s ^ bit)) for s in range(space_count)]
        return lax.ppermute(x, ("snap", "space"), pairs)

    def over_space(keep, send):
        for step in range(len(bits) - 1):
            both = keep + exchanged(send, step)
            half = both.shape[0] // 2
            keep, send = both[:half], both[half:]
        return keep, exchanged(send, len(bits) - 1)

    sums = (*over_space(first_keep, first_send), *over_space(second_keep, second_send))
    summed = pl.pallas_call(
        functools.partial(joined_kernel, width),
        out_shape=jax.ShapeDtypeStruct((chip_count, part_rows, band * width), jnp.float32),
        in_specs=[smem, smem] + [vmem] * 4,
        out_specs=vmem,
        cost_estimate=pl.CostEstimate(flops=1000, bytes_accessed=0, transcendentals=0),
        compiler_params=pltpu.CompilerParams(vmem_limit_bytes=8 << 20),
        name="joined",
    )(early_table, late_table, *sums)

    is_hub = (me >= hubs[0]) & (me <= hubs[-1])
    gram_band = jnp.where(is_hub, summed[0], 0.0)
    for offset in range(1, chip_count):
        gram_band = gram_band + lax.ppermute(summed[offset], "snap", [(h, h ^ (2 * offset)) for h in hubs])
    return gram_band * (1.0 / (row_count * space_count)), mean_field


def solution(mesh):
    return jax.shard_map(
        per_device,
        mesh=mesh,
        in_specs=(P("space", "snap"),),
        out_specs=(P(("snap", "space"), None), P("space")),
        check_vma=False,
    )
```

```python
import functools

import jax
import jax.numpy as jnp
import numpy as np
from jax import lax
from jax.experimental import pallas as pl
from jax.experimental.pallas import tpu as pltpu
from jax.sharding import PartitionSpec as P


LANES = 128


def bits_of(count):
    return [1 << n for n in range(count.bit_length() - 1)]


def part_masks(space_count, core):
    bits = bits_of(space_count)
    taken = [bits[(step + core) % len(bits)] for step in range(len(bits))]
    masks = []
    for position in range(space_count):
        mask = 0
        for step, bit in enumerate(taken):
            if position >> (len(bits) - 1 - step) & 1:
                mask |= bit
        masks.append(mask)
    return masks


def tile_tables(snap_count, late, early):
    chip_count = snap_count // 2
    near = 2 * len(early)
    column = {offset: n for n, offset in enumerate(early)}
    early_rows, late_rows = [], []
    for me in range(snap_count):
        parts = ([], [])
        for offset in range(chip_count):
            block = ((me // 2) ^ offset) * 2 + me % 2
            for k in range(chip_count + 1):
                rel = ((block + k) % snap_count) ^ me
                if offset == late:
                    place = near + 1 if rel == 2 * late + 1 else near if rel == 2 * late else 2 * column[rel // 2] + rel % 2
                    parts[1].append((near + place, offset, k))
                elif rel // 2 == late:
                    parts[1].append((2 * column[offset] + rel % 2, offset, k))
                else:
                    parts[0].append((column[offset] * near + 2 * column[rel // 2] + rel % 2, offset, k))
        early_rows.append(parts[0])
        late_rows.append(parts[1])

    def even(rows):
        longest = max(len(row) for row in rows)
        return np.array([row + [row[-1]] * (longest - len(row)) for row in rows], np.int32).reshape(snap_count, -1)

    return even(early_rows), even(late_rows)


def place_tiles(table_ref, tiles_ref, keep_ref, send_ref):
    me, space = lax.axis_index("snap"), lax.axis_index("space")
    half, slots, part_rows, _ = keep_ref.shape
    core = me % 2
    masks = [part_masks(2 * half, c) for c in (0, 1)]

    def one(slot, carry):
        tile = table_ref[me, 3 * slot]
        for position in range(2 * half):
            part = space ^ jnp.where(core == 0, masks[0][position], masks[1][position])
            rows = pl.ds(pl.multiple_of(part * part_rows, part_rows), part_rows)
            target = keep_ref if position < half else send_ref
            target[position % half, slot] = tiles_ref[tile, rows, :]
        return carry

    lax.fori_loop(0, slots, one, 0)


def as_column(row):
    return jnp.transpose(jnp.broadcast_to(row, (LANES, LANES)))


def product(left, right):
    return lax.dot_general(left, right, (((1,), (0,)), ((), ())), preferred_element_type=jnp.float32)


def split_kernel(hub_of, offsets, rows_ref, *refs):
    pieces, sums_ref, sems = refs[:-2], refs[-2], refs[-1]
    me = lax.axis_index("snap")
    copies = []
    for n, offset in enumerate(offsets):
        first = pl.multiple_of(hub_of(me ^ (2 * offset)), pieces[0].shape[0])
        copies.append(pltpu.make_async_copy(rows_ref.at[pl.ds(first, pieces[0].shape[0]), :], pieces[n], sems.at[n]))
    for copy in reversed(copies):
        copy.start()
    copies[-1].wait()
    for tile in range(sums_ref.shape[0]):
        values = pieces[-1][tile * LANES : (tile + 1) * LANES, :].astype(jnp.float32)
        sums_ref[tile : tile + 1, :] = jnp.sum(jnp.transpose(values), axis=0, keepdims=True)
    for copy in copies[:-1]:
        copy.wait()


def early_kernel(total_columns, table_ref, late_same_ref, late_other_ref, *refs):
    near = len(refs) - 6
    blocks = refs[:near]
    turned_ref, mean_ref, keep_ref, send_ref, fluct_ref, tiles_ref = refs[near:]
    rows, width = blocks[0].shape

    def one_tile(tile, carry):
        target = pl.ds(pl.multiple_of(tile * LANES, LANES), LANES)
        held = [ref[target, :].astype(jnp.float32) for ref in blocks]
        near_sum = jnp.sum(functools.reduce(jnp.add, held), axis=1, keepdims=True)
        far_sum = late_same_ref[pl.ds(tile, 1), :] + late_other_ref[pl.ds(tile, 1), :]
        mean = (as_column(far_sum) + near_sum) * (1.0 / total_columns)
        mean_ref[pl.ds(tile, 1), :] = jnp.transpose(mean)[0:1, :]
        for n in range(near):
            value = (held[n] - mean).astype(jnp.bfloat16)
            fluct_ref[target, n * width : (n + 1) * width] = value
            turned_ref[n * width : (n + 1) * width, target] = jnp.transpose(value)
        return carry

    lax.fori_loop(0, rows // LANES, one_tile, 0)
    for n in range(near // 2):
        left = turned_ref[2 * n * width : (2 * n + 1) * width, :]
        for first in range(0, near, 2):
            both = product(left, fluct_ref[:, first * width : (first + 2) * width])
            tiles_ref[n * near + first] = both[:, :width]
            tiles_ref[n * near + first + 1] = both[:, width:]
    place_tiles(table_ref, tiles_ref, keep_ref, send_ref)


def late_kernel(table_ref, mean_ref, same_ref, other_ref, turned_ref, *refs):
    keep_ref, send_ref, fluct_ref, fluct_turned_ref, tiles_ref = refs
    rows, width = same_ref.shape
    near = turned_ref.shape[0] // width

    def one_tile(tile, carry):
        mean = as_column(mean_ref[pl.ds(tile, 1), :])
        target = pl.ds(pl.multiple_of(tile * LANES, LANES), LANES)
        for n, ref in enumerate((same_ref, other_ref)):
            value = (ref[target, :].astype(jnp.float32) - mean).astype(jnp.bfloat16)
            fluct_ref[target, n * width : (n + 1) * width] = value
            fluct_turned_ref[n * width : (n + 1) * width, target] = jnp.transpose(value)
        return carry

    lax.fori_loop(0, rows // LANES, one_tile, 0)
    step = 2 * width
    for first in range(0, near + 2, 2):
        left = turned_ref[first * width : first * width + step, :] if first < near else fluct_turned_ref[...]
        four = product(left, fluct_ref[...])
        tiles_ref[near + first] = jnp.transpose(four[:width, :width])
        tiles_ref[near + first + 1] = jnp.transpose(four[width:, :width])
        if first < near:
            tiles_ref[first] = four[:width, :width]
            tiles_ref[first + 1] = four[:width, width:]
    place_tiles(table_ref, tiles_ref, keep_ref, send_ref)


def joined_kernel(early_ref, late_ref, mean_ref, first_keep, first_recv, second_keep, second_recv, out_ref):
    me = lax.axis_index("snap")
    _, _, part_rows, width = first_keep.shape
    for table, keep, recv in ((early_ref, first_keep, first_recv), (late_ref, second_keep, second_recv)):

        def one(slot, carry, table=table, keep=keep, recv=recv):
            offset, k = table[me, 3 * slot + 1], table[me, 3 * slot + 2]
            lanes = pl.ds(pl.multiple_of(k * width, width), width)
            out_ref[offset, 0:part_rows, lanes] = keep[0, slot] + recv[0, slot]
            return carry

        lax.fori_loop(0, keep.shape[1], one, 0)
    band = out_ref.shape[2] // width
    for offset in range(out_ref.shape[0]):
        for n in range(mean_ref.shape[0]):
            row = part_rows + n // band
            out_ref[offset, row : row + 1, (n % band) * width : (n % band + 1) * width] = mean_ref[n : n + 1, :]


def collected_kernel(first_chip, scale, own_ref, *refs):
    others, (gram_ref, mean_ref) = refs[:-2], refs[-2:]
    chip = lax.axis_index("snap") // 2
    part_rows, columns = gram_ref.shape
    chip_count = len(others) + 1
    hub_chips = chip_count // 2
    is_hub = (chip >= first_chip) & (chip < first_chip + hub_chips)
    total = jnp.where(is_hub, own_ref[0:part_rows, :], 0.0)
    for ref in others:
        total = total + ref[0:part_rows, :]
    gram_ref[...] = total * scale
    slabs = (own_ref, *others)
    mean_rows = mean_ref.shape[0] // hub_chips
    band = columns // LANES
    for offset, ref in enumerate(slabs):
        hub = (chip ^ offset) - first_chip

        @pl.when((hub >= 0) & (hub < hub_chips))
        def _(ref=ref, hub=hub):
            for n in range(mean_rows):
                row = part_rows + n // band
                mean_ref[pl.ds(hub * mean_rows + n, 1), :] = ref[row : row + 1, (n % band) * LANES : (n % band + 1) * LANES]


def per_device(snapshots):
    snap_count = lax.axis_size("snap")
    space_count = lax.axis_size("space")
    row_count, width = snapshots.shape
    chip_count = snap_count // 2
    first_chip, hub_chips = chip_count // 4, chip_count // 2
    hubs = list(range(2 * first_chip, 2 * (first_chip + hub_chips)))
    rows = row_count // hub_chips
    band = chip_count + 1
    part_rows = width // space_count
    late = chip_count // 2
    early = [offset for offset in range(chip_count) if offset != late]
    near = 2 * len(early)
    smem = pl.BlockSpec(memory_space=pltpu.SMEM)
    vmem = pl.BlockSpec(memory_space=pltpu.VMEM)

    def shaped(dtype, *shape):
        return jax.ShapeDtypeStruct(shape, dtype)

    def kernel(body, tables, operands, out_shapes, scratch=(), flops=1000, raw=False):
        sizes = [int(np.prod(s.shape)) * jnp.dtype(s.dtype).itemsize for s in (*operands, *out_shapes)]
        sizes += [int(np.prod(s.shape)) * jnp.dtype(s.dtype).itemsize for s in scratch if hasattr(s, "shape") and s.memory_space == pltpu.VMEM]
        return pl.pallas_call(
            body,
            out_shape=list(out_shapes),
            in_specs=[smem] * len(tables) + [pl.BlockSpec(memory_space=pl.ANY) if raw else vmem] * len(operands),
            out_specs=[vmem] * len(out_shapes),
            scratch_shapes=list(scratch),
            cost_estimate=pl.CostEstimate(flops=flops, bytes_accessed=0, transcendentals=0),
            compiler_params=pltpu.CompilerParams(vmem_limit_bytes=(60 << 20) if raw else sum(sizes) + (6 << 20)),
        )(*tables, *operands)

    def hub_of(device):
        return jnp.clip(device // 2 - first_chip, 0, hub_chips - 1) * rows

    def to_hubs(x, offset):
        return lax.ppermute(x, "snap", [(h ^ (2 * offset), h) for h in hubs])

    def to_other_core(x):
        return lax.ppermute(x, "snap", [(h, h ^ 1) for h in hubs])

    piece = shaped(snapshots.dtype, rows, width)
    sums = shaped(jnp.float32, rows // LANES, LANES)
    offsets = early + [late]
    *pieces, far_sums = kernel(
        functools.partial(split_kernel, hub_of, offsets),
        [],
        [snapshots],
        [piece] * chip_count + [sums],
        [pltpu.SemaphoreType.DMA((chip_count,))],
        raw=True,
    )
    late_same = to_hubs(far_sums, late)
    blocks = {0: pieces[0]}
    for offset, x in zip(offsets[1:], pieces[1:]):
        blocks[offset] = to_hubs(x, offset)
    late_other = to_other_core(late_same)
    passed = {offset: to_other_core(blocks[offset]) for offset in offsets}

    early_all, late_all = tile_tables(snap_count, late, early)
    early_table, late_table = jnp.asarray(early_all), jnp.asarray(late_all)

    def halves(table):
        return [shaped(jnp.float32, space_count // 2, table.shape[1] // 3, part_rows, width)] * 2

    operands = [late_same, late_other]
    for offset in early:
        operands += [blocks[offset], passed[offset]]
    turned, mean_rows, first_keep, first_send = kernel(
        functools.partial(early_kernel, width * snap_count),
        [early_table],
        operands,
        [shaped(jnp.bfloat16, near * width, rows), sums] + halves(early_all),
        [pltpu.VMEM((rows, near * width), jnp.bfloat16), pltpu.VMEM((near * near // 2, width, width), jnp.float32)],
        flops=near * near * width * width * rows,
    )
    second_keep, second_send = kernel(
        late_kernel,
        [late_table],
        [mean_rows, blocks[late], passed[late], turned],
        halves(late_all),
        [
            pltpu.VMEM((rows, 2 * width), jnp.bfloat16),
            pltpu.VMEM((2 * width, rows), jnp.bfloat16),
            pltpu.VMEM((2 * near + 2, width, width), jnp.float32),
        ],
        flops=4 * snap_count * width * width * rows,
    )

    bits = bits_of(space_count)

    def exchanged(x, step):
        pairs = []
        for h in hubs:
            bit = bits[(step + h % 2) % len(bits)]
            pairs += [(h * space_count + s, h * space_count + (s ^ bit)) for s in range(space_count)]
        return lax.ppermute(x, ("snap", "space"), pairs)

    def over_space(keep, send):
        for step in range(len(bits) - 1):
            both = keep + exchanged(send, step)
            half = both.shape[0] // 2
            keep, send = both[:half], both[half:]
        return keep, exchanged(send, len(bits) - 1)

    summed = (*over_space(first_keep, first_send), *over_space(second_keep, second_send))
    mean_space = -(-(-(-(rows // LANES) // band)) // 8) * 8
    slab = shaped(jnp.float32, part_rows + mean_space, band * width)
    (slabs,) = kernel(
        joined_kernel, [early_table, late_table], [mean_rows, *summed], [shaped(jnp.float32, chip_count, *slab.shape)]
    )

    own = [slabs[0]]
    for offset in range(1, chip_count):
        own.append(lax.ppermute(slabs[offset], "snap", [(h, h ^ (2 * offset)) for h in hubs]))
    gram_band, mean_field = kernel(
        functools.partial(collected_kernel, first_chip, 1.0 / (row_count * space_count)),
        [],
        own,
        [shaped(jnp.float32, part_rows, band * width), shaped(jnp.float32, row_count // LANES, LANES)],
    )
    return gram_band, mean_field.reshape(row_count)


def solution(mesh):
    return jax.shard_map(
        per_device,
        mesh=mesh,
        in_specs=(P("space", "snap"),),
        out_specs=(P(("snap", "space"), None), P("space")),
        check_vma=False,
    )
```

```python
import functools

import jax
import jax.numpy as jnp
import numpy as np
from jax import lax
from jax.experimental import pallas as pl
from jax.experimental.pallas import tpu as pltpu
from jax.sharding import PartitionSpec as P


LANES = 128


def completed(pairs, count):
    sources = [i for i in range(count) if i not in {p[0] for p in pairs}]
    targets = [i for i in range(count) if i not in {p[1] for p in pairs}]
    same = [i for i in sources if i in targets]
    left = zip([i for i in sources if i not in same], [i for i in targets if i not in same])
    return list(pairs) + [(i, i) for i in same] + list(left)


def place_tiles(wanted_late, tile_of, out_refs):
    me, space = lax.axis_index("snap"), lax.axis_index("space")
    snap_count = lax.axis_size("snap")
    chip_count, late = snap_count // 2, snap_count // 4
    band = chip_count + 1
    part_rows = out_refs[0].shape[1]

    def one(pair, slot):
        offset, k = pair // band, pair % band
        block = ((me // 2) ^ offset) * 2 + me % 2
        rel = ((block + k) % snap_count) ^ me
        is_late = jnp.logical_or(offset == late, rel // 2 == late)
        wanted = is_late if wanted_late else jnp.logical_not(is_late)

        @pl.when(wanted)
        def _():
            for n, out_ref in enumerate(out_refs):
                rows = pl.ds(pl.multiple_of((space ^ n) * part_rows, part_rows), part_rows)
                out_ref[slot] = tile_of(offset, rel, rows)

        return slot + jnp.where(wanted, 1, 0)

    lax.fori_loop(0, chip_count * band, one, 0)


def slot_count(snap_count, wanted_late):
    chip_count, late = snap_count // 2, snap_count // 4
    counts = []
    for me in range(snap_count):
        count = 0
        for offset in range(chip_count):
            block = ((me // 2) ^ offset) * 2 + me % 2
            for k in range(chip_count + 1):
                rel = ((block + k) % snap_count) ^ me
                count += (late in (offset, rel // 2)) == wanted_late
        counts.append(count)
    return max(counts)


def as_column(row):
    return jnp.transpose(jnp.broadcast_to(row, (LANES, LANES)))


def product(left, right):
    return lax.dot_general(left, right, (((1,), (0,)), ((), ())), preferred_element_type=jnp.float32)


def split_kernel(hub_of, offsets, rows_ref, *refs):
    pieces, sems = refs[:-1], refs[-1]
    me = lax.axis_index("snap")
    copies = []
    for n, offset in enumerate(offsets):
        first = pl.multiple_of(hub_of(me ^ (2 * offset)), pieces[0].shape[0])
        copies.append(pltpu.make_async_copy(rows_ref.at[pl.ds(first, pieces[0].shape[0]), :], pieces[n], sems.at[n]))
    for copy in copies:
        copy.start()
    for copy in copies:
        copy.wait()


def sums_kernel(piece_ref, sums_ref):
    for tile in range(sums_ref.shape[0]):
        values = piece_ref[tile * LANES : (tile + 1) * LANES, :].astype(jnp.float32)
        sums_ref[tile : tile + 1, :] = jnp.sum(jnp.transpose(values), axis=0, keepdims=True)


def early_kernel(total_columns, near, late_same_ref, late_other_ref, *refs):
    blocks = refs[:near]
    turned_ref, mean_ref, spread_ref, *out_refs = refs[near:-2]
    fluct_ref, tiles_ref = refs[-2:]
    rows, width = blocks[0].shape

    def one_tile(tile, carry):
        target = pl.ds(pl.multiple_of(tile * LANES, LANES), LANES)
        held = [ref[target, :].astype(jnp.float32) for ref in blocks]
        near_sum = jnp.sum(jnp.transpose(functools.reduce(jnp.add, held)), axis=0, keepdims=True)
        far_sum = late_same_ref[pl.ds(tile, 1), :] + late_other_ref[pl.ds(tile, 1), :]
        row = (near_sum + far_sum) * (1.0 / total_columns)
        mean_ref[pl.ds(tile, 1), :] = row
        mean = as_column(row)
        spread_ref[target, :] = mean
        for n in range(near):
            value = (held[n] - mean).astype(jnp.bfloat16)
            fluct_ref[target, n * width : (n + 1) * width] = value
            turned_ref[n * width : (n + 1) * width, target] = jnp.transpose(value)
        return carry

    lax.fori_loop(0, rows // LANES, one_tile, 0)
    half = near // 2
    for first in range(0, near * width, 2 * width):
        columns = slice(first, min(first + 2 * width, near * width))
        tiles_ref[:, columns] = product(turned_ref[0 : half * width, :], fluct_ref[:, columns])
    late = lax.axis_size("snap") // 4

    def tile_of(offset, rel, rows):
        other = rel // 2
        row = offset - jnp.where(offset > late, 1, 0)
        column = other - jnp.where(other > late, 1, 0) + half * (rel % 2)
        rows = pl.ds(pl.multiple_of(row * width + rows.start, rows.size), rows.size)
        return tiles_ref[rows, pl.ds(pl.multiple_of(column * width, width), width)]

    place_tiles(False, tile_of, out_refs)


def late_kernel(near, spread_ref, same_ref, other_ref, turned_ref, *refs):
    out_refs, (fluct_ref, far_turned_ref, tiles_ref) = refs[:-3], refs[-3:]
    rows, width = same_ref.shape

    def one_tile(tile, carry):
        target = pl.ds(pl.multiple_of(tile * LANES, LANES), LANES)
        mean = spread_ref[target, :]
        for n, ref in enumerate((same_ref, other_ref)):
            value = (ref[target, :].astype(jnp.float32) - mean).astype(jnp.bfloat16)
            fluct_ref[target, n * width : (n + 1) * width] = value
            far_turned_ref[n * width : (n + 1) * width, target] = jnp.transpose(value)
        return carry

    lax.fori_loop(0, rows // LANES, one_tile, 0)
    half = near // 2
    step = half * width
    for first in range(0, near * width, step):
        with_far = product(turned_ref[first : first + step, :], fluct_ref[...])
        for n in range(half):
            place = first // width + n
            tile = with_far[n * width : (n + 1) * width, :]
            tiles_ref[place] = jnp.transpose(tile[:, :width])
            if first == 0:
                tiles_ref[near + 2 + 2 * n] = tile[:, :width]
                tiles_ref[near + 3 + 2 * n] = tile[:, width:]
    both = product(far_turned_ref[...], fluct_ref[...])
    tiles_ref[near] = both[:width, :width]
    tiles_ref[near + 1] = jnp.transpose(both[width:, :width])
    late = lax.axis_size("snap") // 4

    def tile_of(offset, rel, rows):
        other = rel // 2
        row = offset - jnp.where(offset > late, 1, 0)
        column = other - jnp.where(other > late, 1, 0) + half * (rel % 2)
        turned = jnp.where(other == late, near + rel % 2, column)
        place = jnp.where(offset == late, turned, near + 2 + 2 * row + rel % 2)
        return tiles_ref[place, rows, :]

    place_tiles(True, tile_of, out_refs)


def joined_kernel(space_count, mean_ref, *refs):
    firsts, seconds, out_refs = refs[:space_count], refs[space_count : 2 * space_count], refs[2 * space_count :]
    me = lax.axis_index("snap")
    snap_count = lax.axis_size("snap")
    chip_count, late = snap_count // 2, snap_count // 4
    band = chip_count + 1
    _, part_rows, width = firsts[0].shape
    for offset, out_ref in enumerate(out_refs):
        if offset == 0:
            first_slot, second_slot = 0, 0
        block = ((me // 2) ^ offset) * 2 + me % 2
        for k in range(band):
            rel = ((block + k) % snap_count) ^ me
            is_late = jnp.logical_or(offset == late, rel // 2 == late)
            lanes = slice(k * width, (k + 1) * width)

            @pl.when(is_late)
            def _(out_ref=out_ref, lanes=lanes, slot=second_slot):
                out_ref[0:part_rows, lanes] = functools.reduce(jnp.add, [ref[slot] for ref in seconds])

            @pl.when(jnp.logical_not(is_late))
            def _(out_ref=out_ref, lanes=lanes, slot=first_slot):
                out_ref[0:part_rows, lanes] = functools.reduce(jnp.add, [ref[slot] for ref in firsts])

            second_slot = second_slot + jnp.where(is_late, 1, 0)
            first_slot = first_slot + jnp.where(is_late, 0, 1)
        for n in range(mean_ref.shape[0]):
            row = part_rows + n // band
            out_ref[row : row + 1, (n % band) * width : (n % band + 1) * width] = mean_ref[n : n + 1, :]


def collected_kernel(first_chip, scale, own_ref, *refs):
    others, (gram_ref, mean_ref) = refs[:-2], refs[-2:]
    chip = lax.axis_index("snap") // 2
    part_rows, columns = gram_ref.shape
    chip_count = len(others) + 1
    hub_chips = chip_count // 2
    slabs = (own_ref, *others)
    total = jnp.zeros((part_rows, columns), jnp.float32)
    for offset, ref in enumerate(slabs):
        hub = (chip ^ offset) - first_chip
        total = total + jnp.where((hub >= 0) & (hub < hub_chips), ref[0:part_rows, :], 0.0)
    gram_ref[...] = total * scale
    mean_rows = mean_ref.shape[0] // hub_chips
    band = columns // LANES
    for offset, ref in enumerate(slabs):
        hub = (chip ^ offset) - first_chip

        @pl.when((hub >= 0) & (hub < hub_chips))
        def _(ref=ref, hub=hub):
            for n in range(mean_rows):
                row = part_rows + n // band
                mean_ref[pl.ds(hub * mean_rows + n, 1), :] = ref[row : row + 1, (n % band) * LANES : (n % band + 1) * LANES]


def per_device(snapshots):
    snap_count = lax.axis_size("snap")
    space_count = lax.axis_size("space")
    row_count, width = snapshots.shape
    chip_count = snap_count // 2
    first_chip, hub_chips = chip_count // 4, chip_count // 2
    hubs = list(range(2 * first_chip, 2 * (first_chip + hub_chips)))
    rows = row_count // hub_chips
    band = chip_count + 1
    part_rows = width // space_count
    late = chip_count // 2
    early = [offset for offset in range(chip_count) if offset != late]
    near = 2 * len(early)
    vmem = pl.BlockSpec(memory_space=pltpu.VMEM)

    def shaped(dtype, *shape):
        return jax.ShapeDtypeStruct(shape, dtype)

    def kernel(body, operands, out_shapes, scratch=(), flops=1000, raw=False):
        sizes = [int(np.prod(s.shape)) * jnp.dtype(s.dtype).itemsize for s in (*operands, *out_shapes)]
        sizes += [int(np.prod(s.shape)) * jnp.dtype(s.dtype).itemsize for s in scratch if hasattr(s, "shape") and s.memory_space == pltpu.VMEM]
        return pl.pallas_call(
            body,
            out_shape=list(out_shapes),
            in_specs=[pl.BlockSpec(memory_space=pltpu.HBM) if raw else vmem] * len(operands),
            out_specs=[vmem] * len(out_shapes),
            scratch_shapes=list(scratch),
            cost_estimate=pl.CostEstimate(flops=flops, bytes_accessed=0, transcendentals=0),
            compiler_params=pltpu.CompilerParams(vmem_limit_bytes=sum(sizes) + (6 << 20)),
        )(*operands)

    def hub_of(device):
        return jnp.clip(device // 2 - first_chip, 0, hub_chips - 1) * rows

    def to_hubs(x, offset, name):
        pairs = [(h ^ (2 * offset), h) for h in hubs]
        full = name == "sums" or all(h ^ (2 * offset) in hubs for h in hubs)
        return lax.ppermute(x, "snap", completed(pairs, snap_count) if full else pairs)

    def to_other_core(x):
        return lax.ppermute(x, "snap", [(i, i ^ 1) for i in range(snap_count)])

    piece = shaped(snapshots.dtype, rows, width)
    sums = shaped(jnp.float32, rows // LANES, LANES)
    offsets = early + [late]
    pieces = kernel(
        functools.partial(split_kernel, hub_of, offsets),
        [snapshots],
        [piece] * chip_count,
        [pltpu.SemaphoreType.DMA((chip_count,))],
        raw=True,
    )
    (far_sums,) = kernel(sums_kernel, [pieces[-1]], [sums])
    late_same = to_hubs(far_sums, late, "sums")
    blocks = {0: pieces[0]}
    for offset, x in zip(offsets[1:], pieces[1:]):
        blocks[offset] = to_hubs(x, offset, "bulk")
    late_other = to_other_core(late_same)
    passed = {offset: to_other_core(blocks[offset]) for offset in offsets}

    first_slots, second_slots = slot_count(snap_count, False), slot_count(snap_count, True)
    turned, mean_rows, spread, *first = kernel(
        functools.partial(early_kernel, width * snap_count, near),
        [late_same, late_other] + [blocks[offset] for offset in early] + [passed[offset] for offset in early],
        [shaped(jnp.bfloat16, near * width, rows), sums, shaped(jnp.float32, rows, LANES)]
        + [shaped(jnp.float32, first_slots, part_rows, width)] * space_count,
        [pltpu.VMEM((rows, near * width), jnp.bfloat16), pltpu.VMEM((near // 2 * width, near * width), jnp.float32)],
        flops=near * near * width * width * rows,
    )
    second = kernel(
        functools.partial(late_kernel, near),
        [spread, blocks[late], passed[late], turned],
        [shaped(jnp.float32, second_slots, part_rows, width)] * space_count,
        [
            pltpu.VMEM((rows, 2 * width), jnp.bfloat16),
            pltpu.VMEM((2 * width, rows), jnp.bfloat16),
            pltpu.VMEM((2 * near + 2, width, width), jnp.float32),
        ],
        flops=4 * snap_count * width * width * rows,
    )

    def over_space(parts):
        got = [parts[0]]
        for n in range(1, space_count):
            got.append(lax.ppermute(parts[n], "space", [(s, s ^ n) for s in range(space_count)]))
        return got

    mean_space = -(-(-(-(rows // LANES) // band)) // 8) * 8
    slab = shaped(jnp.float32, part_rows + mean_space, band * width)
    slabs = kernel(
        functools.partial(joined_kernel, space_count),
        [mean_rows, *over_space(first), *over_space(second)],
        [slab] * chip_count,
    )

    own = [slabs[0]]
    for offset in range(1, chip_count):
        pairs = completed([(h, h ^ (2 * offset)) for h in hubs], snap_count)
        own.append(lax.ppermute(slabs[offset], "snap", pairs))
    gram_band, mean_field = kernel(
        functools.partial(collected_kernel, first_chip, 1.0 / (row_count * space_count)),
        own,
        [shaped(jnp.float32, part_rows, band * width), shaped(jnp.float32, row_count // LANES, LANES)],
    )
    return gram_band, mean_field.reshape(row_count)


def solution(mesh):
    return jax.shard_map(
        per_device,
        mesh=mesh,
        in_specs=(P("space", "snap"),),
        out_specs=(P(("snap", "space"), None), P("space")),
        check_vma=False,
    )
```

```python
import functools
import math

import jax
import jax.numpy as jnp
import numpy as np
from jax import lax
from jax.experimental import pallas as pl
from jax.experimental.pallas import tpu as pltpu
from jax.sharding import PartitionSpec as P


LANES = 128


def completed(pairs, count):
    sources = [i for i in range(count) if i not in {p[0] for p in pairs}]
    targets = [i for i in range(count) if i not in {p[1] for p in pairs}]
    same = [i for i in sources if i in targets]
    left = zip([i for i in sources if i not in same], [i for i in targets if i not in same])
    return list(pairs) + [(i, i) for i in same] + list(left)


def place_tiles(wanted_late, tile_of, out_refs):
    me, space = lax.axis_index("snap"), lax.axis_index("space")
    snap_count = lax.axis_size("snap")
    chip_count, late = snap_count // 2, snap_count // 4
    band = chip_count + 1
    part_rows = out_refs[0].shape[1]

    def one(pair, slot):
        offset, k = pair // band, pair % band
        block = ((me // 2) ^ offset) * 2 + me % 2
        rel = ((block + k) % snap_count) ^ me
        is_late = jnp.logical_or(offset == late, rel // 2 == late)
        wanted = is_late if wanted_late else jnp.logical_not(is_late)

        @pl.when(wanted)
        def _():
            for n, out_ref in enumerate(out_refs):
                rows = pl.ds(pl.multiple_of((space ^ n) * part_rows, part_rows), part_rows)
                out_ref[slot] = tile_of(offset, rel, rows)

        return slot + jnp.where(wanted, 1, 0)

    lax.fori_loop(0, chip_count * band, one, 0)


def slot_count(snap_count, wanted_late):
    chip_count, late = snap_count // 2, snap_count // 4
    counts = []
    for me in range(snap_count):
        count = 0
        for offset in range(chip_count):
            block = ((me // 2) ^ offset) * 2 + me % 2
            for k in range(chip_count + 1):
                rel = ((block + k) % snap_count) ^ me
                count += (late in (offset, rel // 2)) == wanted_late
        counts.append(count)
    return max(counts)


def as_column(row):
    return jnp.transpose(jnp.broadcast_to(row, (LANES, LANES)))


def product(left, right):
    return lax.dot_general(left, right, (((1,), (0,)), ((), ())), preferred_element_type=jnp.float32)


def over_tiles(count, one_tile):
    group = math.gcd(count, 4)

    def some(step, carry):
        for n in range(group):
            one_tile(step * group + n)
        return carry

    lax.fori_loop(0, count // group, some, 0)


def split_kernel(hub_of, offsets, rows_ref, *refs):
    pieces, sems = refs[:-1], refs[-1]
    me = lax.axis_index("snap")
    copies = []
    for n, offset in enumerate(offsets):
        first = pl.multiple_of(hub_of(me ^ (2 * offset)), pieces[0].shape[0])
        copies.append(pltpu.make_async_copy(rows_ref.at[pl.ds(first, pieces[0].shape[0]), :], pieces[n], sems.at[n]))
    for copy in copies:
        copy.start()
    for copy in copies:
        copy.wait()


def sums_kernel(piece_ref, sums_ref):
    for tile in range(sums_ref.shape[0]):
        values = piece_ref[tile * LANES : (tile + 1) * LANES, :].astype(jnp.float32)
        sums_ref[tile : tile + 1, :] = jnp.sum(jnp.transpose(values), axis=0, keepdims=True)


def early_kernel(total_columns, near, late_same_ref, late_other_ref, *refs):
    blocks = refs[:near]
    turned_ref, mean_ref, spread_ref, *out_refs = refs[near:-2]
    fluct_ref, tiles_ref = refs[-2:]
    rows, width = blocks[0].shape

    def one_tile(tile):
        target = pl.ds(pl.multiple_of(tile * LANES, LANES), LANES)
        held = [ref[target, :].astype(jnp.float32) for ref in blocks]
        near_sum = jnp.sum(jnp.transpose(functools.reduce(jnp.add, held)), axis=0, keepdims=True)
        far_sum = late_same_ref[pl.ds(tile, 1), :] + late_other_ref[pl.ds(tile, 1), :]
        row = (near_sum + far_sum) * (1.0 / total_columns)
        mean_ref[pl.ds(tile, 1), :] = row
        mean = as_column(row)
        spread_ref[target, :] = mean
        for n in range(near):
            value = (held[n] - mean).astype(jnp.bfloat16)
            fluct_ref[target, n * width : (n + 1) * width] = value
            turned_ref[n * width : (n + 1) * width, target] = jnp.transpose(value)

    over_tiles(rows // LANES, one_tile)
    half = near // 2
    for first in range(0, near * width, 2 * width):
        columns = slice(first, min(first + 2 * width, near * width))
        tiles_ref[:, columns] = product(turned_ref[0 : half * width, :], fluct_ref[:, columns])
    late = lax.axis_size("snap") // 4

    def tile_of(offset, rel, rows):
        other = rel // 2
        row = offset - jnp.where(offset > late, 1, 0)
        column = other - jnp.where(other > late, 1, 0) + half * (rel % 2)
        rows = pl.ds(pl.multiple_of(row * width + rows.start, rows.size), rows.size)
        return tiles_ref[rows, pl.ds(pl.multiple_of(column * width, width), width)]

    place_tiles(False, tile_of, out_refs)


def late_kernel(near, spread_ref, same_ref, other_ref, turned_ref, *refs):
    out_refs, (fluct_ref, far_turned_ref, tiles_ref) = refs[:-3], refs[-3:]
    rows, width = same_ref.shape

    def one_tile(tile):
        target = pl.ds(pl.multiple_of(tile * LANES, LANES), LANES)
        mean = spread_ref[target, :]
        for n, ref in enumerate((same_ref, other_ref)):
            value = (ref[target, :].astype(jnp.float32) - mean).astype(jnp.bfloat16)
            fluct_ref[target, n * width : (n + 1) * width] = value
            far_turned_ref[n * width : (n + 1) * width, target] = jnp.transpose(value)

    over_tiles(rows // LANES, one_tile)
    half = near // 2
    step = half * width
    for first in range(0, near * width, step):
        with_far = product(turned_ref[first : first + step, :], fluct_ref[...])
        for n in range(half):
            place = first // width + n
            tile = with_far[n * width : (n + 1) * width, :]
            tiles_ref[place] = jnp.transpose(tile[:, :width])
            if first == 0:
                tiles_ref[near + 2 + 2 * n] = tile[:, :width]
                tiles_ref[near + 3 + 2 * n] = tile[:, width:]
    both = product(far_turned_ref[...], fluct_ref[...])
    tiles_ref[near] = both[:width, :width]
    tiles_ref[near + 1] = jnp.transpose(both[width:, :width])
    late = lax.axis_size("snap") // 4

    def tile_of(offset, rel, rows):
        other = rel // 2
        row = offset - jnp.where(offset > late, 1, 0)
        column = other - jnp.where(other > late, 1, 0) + half * (rel % 2)
        turned = jnp.where(other == late, near + rel % 2, column)
        place = jnp.where(offset == late, turned, near + 2 + 2 * row + rel % 2)
        return tiles_ref[place, rows, :]

    place_tiles(True, tile_of, out_refs)


def joined_kernel(space_count, mean_ref, *refs):
    firsts, seconds, out_refs = refs[:space_count], refs[space_count : 2 * space_count], refs[2 * space_count :]
    me = lax.axis_index("snap")
    snap_count = lax.axis_size("snap")
    chip_count, late = snap_count // 2, snap_count // 4
    band = chip_count + 1
    _, part_rows, width = firsts[0].shape
    for offset, out_ref in enumerate(out_refs):
        if offset == 0:
            first_slot, second_slot = 0, 0
        block = ((me // 2) ^ offset) * 2 + me % 2
        for k in range(band):
            rel = ((block + k) % snap_count) ^ me
            is_late = jnp.logical_or(offset == late, rel // 2 == late)
            lanes = slice(k * width, (k + 1) * width)

            @pl.when(is_late)
            def _(out_ref=out_ref, lanes=lanes, slot=second_slot):
                out_ref[0:part_rows, lanes] = functools.reduce(jnp.add, [ref[slot] for ref in seconds])

            @pl.when(jnp.logical_not(is_late))
            def _(out_ref=out_ref, lanes=lanes, slot=first_slot):
                out_ref[0:part_rows, lanes] = functools.reduce(jnp.add, [ref[slot] for ref in firsts])

            second_slot = second_slot + jnp.where(is_late, 1, 0)
            first_slot = first_slot + jnp.where(is_late, 0, 1)
        for n in range(mean_ref.shape[0]):
            row = part_rows + n // band
            out_ref[row : row + 1, (n % band) * width : (n % band + 1) * width] = mean_ref[n : n + 1, :]


def collected_kernel(first_chip, scale, own_ref, *refs):
    others, (gram_ref, mean_ref) = refs[:-2], refs[-2:]
    chip = lax.axis_index("snap") // 2
    part_rows, columns = gram_ref.shape
    chip_count = len(others) + 1
    hub_chips = chip_count // 2
    slabs = (own_ref, *others)
    total = jnp.zeros((part_rows, columns), jnp.float32)
    for offset, ref in enumerate(slabs):
        hub = (chip ^ offset) - first_chip
        total = total + jnp.where((hub >= 0) & (hub < hub_chips), ref[0:part_rows, :], 0.0)
    gram_ref[...] = total * scale
    mean_rows = mean_ref.shape[0] // hub_chips
    band = columns // LANES
    for offset, ref in enumerate(slabs):
        hub = (chip ^ offset) - first_chip

        @pl.when((hub >= 0) & (hub < hub_chips))
        def _(ref=ref, hub=hub):
            for n in range(mean_rows):
                row = part_rows + n // band
                mean_ref[pl.ds(hub * mean_rows + n, 1), :] = ref[row : row + 1, (n % band) * LANES : (n % band + 1) * LANES]


def per_device(snapshots):
    snap_count = lax.axis_size("snap")
    space_count = lax.axis_size("space")
    row_count, width = snapshots.shape
    chip_count = snap_count // 2
    first_chip, hub_chips = chip_count // 4, chip_count // 2
    hubs = list(range(2 * first_chip, 2 * (first_chip + hub_chips)))
    rows = row_count // hub_chips
    band = chip_count + 1
    part_rows = width // space_count
    late = chip_count // 2
    early = [offset for offset in range(chip_count) if offset != late]
    near = 2 * len(early)
    vmem = pl.BlockSpec(memory_space=pltpu.VMEM)

    def shaped(dtype, *shape):
        return jax.ShapeDtypeStruct(shape, dtype)

    def kernel(body, operands, out_shapes, scratch=(), flops=1000, raw=False):
        sizes = [int(np.prod(s.shape)) * jnp.dtype(s.dtype).itemsize for s in (*operands, *out_shapes)]
        sizes += [int(np.prod(s.shape)) * jnp.dtype(s.dtype).itemsize for s in scratch if hasattr(s, "shape") and s.memory_space == pltpu.VMEM]
        return pl.pallas_call(
            body,
            out_shape=list(out_shapes),
            in_specs=[pl.BlockSpec(memory_space=pltpu.HBM) if raw else vmem] * len(operands),
            out_specs=[vmem] * len(out_shapes),
            scratch_shapes=list(scratch),
            cost_estimate=pl.CostEstimate(flops=flops, bytes_accessed=0, transcendentals=0),
            compiler_params=pltpu.CompilerParams(vmem_limit_bytes=sum(sizes) + (6 << 20)),
        )(*operands)

    def hub_of(device):
        return jnp.clip(device // 2 - first_chip, 0, hub_chips - 1) * rows

    def to_hubs(x, offset, name):
        pairs = [(h ^ (2 * offset), h) for h in hubs]
        full = name == "sums" or all(h ^ (2 * offset) in hubs for h in hubs)
        return lax.ppermute(x, "snap", completed(pairs, snap_count) if full else pairs)

    def to_other_core(x):
        return lax.ppermute(x, "snap", [(i, i ^ 1) for i in range(snap_count)])

    piece = shaped(snapshots.dtype, rows, width)
    sums = shaped(jnp.float32, rows // LANES, LANES)
    offsets = early + [late]
    pieces = kernel(
        functools.partial(split_kernel, hub_of, offsets),
        [pltpu.with_memory_space_constraint(snapshots, pltpu.HBM)],
        [piece] * chip_count,
        [pltpu.SemaphoreType.DMA((chip_count,))],
        raw=True,
    )
    (far_sums,) = kernel(sums_kernel, [pieces[-1]], [sums])
    late_same = to_hubs(far_sums, late, "sums")
    blocks = {0: pieces[0]}
    for offset, x in zip(offsets[1:], pieces[1:]):
        blocks[offset] = to_hubs(x, offset, "bulk")
    late_other = to_other_core(late_same)
    passed = {offset: to_other_core(blocks[offset]) for offset in offsets}

    first_slots, second_slots = slot_count(snap_count, False), slot_count(snap_count, True)
    turned, mean_rows, spread, *first = kernel(
        functools.partial(early_kernel, width * snap_count, near),
        [late_same, late_other] + [blocks[offset] for offset in early] + [passed[offset] for offset in early],
        [shaped(jnp.bfloat16, near * width, rows), sums, shaped(jnp.float32, rows, LANES)]
        + [shaped(jnp.float32, first_slots, part_rows, width)] * space_count,
        [pltpu.VMEM((rows, near * width), jnp.bfloat16), pltpu.VMEM((near // 2 * width, near * width), jnp.float32)],
        flops=near * near * width * width * rows,
    )
    second = kernel(
        functools.partial(late_kernel, near),
        [spread, blocks[late], passed[late], turned],
        [shaped(jnp.float32, second_slots, part_rows, width)] * space_count,
        [
            pltpu.VMEM((rows, 2 * width), jnp.bfloat16),
            pltpu.VMEM((2 * width, rows), jnp.bfloat16),
            pltpu.VMEM((2 * near + 2, width, width), jnp.float32),
        ],
        flops=4 * snap_count * width * width * rows,
    )

    def over_space(parts):
        got = [parts[0]]
        for n in range(1, space_count):
            got.append(lax.ppermute(parts[n], "space", [(s, s ^ n) for s in range(space_count)]))
        return got

    mean_space = -(-(-(-(rows // LANES) // band)) // 8) * 8
    slab = shaped(jnp.float32, part_rows + mean_space, band * width)
    slabs = kernel(
        functools.partial(joined_kernel, space_count),
        [mean_rows, *over_space(first), *over_space(second)],
        [slab] * chip_count,
    )

    own = [slabs[0]]
    for offset in range(1, chip_count):
        pairs = completed([(h, h ^ (2 * offset)) for h in hubs], snap_count)
        own.append(lax.ppermute(slabs[offset], "snap", pairs))
    gram_band, mean_field = kernel(
        functools.partial(collected_kernel, first_chip, 1.0 / (row_count * space_count)),
        own,
        [shaped(jnp.float32, part_rows, band * width), shaped(jnp.float32, row_count // LANES, LANES)],
    )
    return gram_band, mean_field.reshape(row_count)


def solution(mesh):
    return jax.shard_map(
        per_device,
        mesh=mesh,
        in_specs=(P("space", "snap"),),
        out_specs=(P(("snap", "space"), None), P("space")),
        check_vma=False,
    )
```

```python
import functools
import math

import jax
import jax.numpy as jnp
import numpy as np
from jax import lax
from jax.experimental import pallas as pl
from jax.experimental.pallas import tpu as pltpu
from jax.sharding import PartitionSpec as P


LANES = 128


def completed(pairs, count):
    sources = [i for i in range(count) if i not in {p[0] for p in pairs}]
    targets = [i for i in range(count) if i not in {p[1] for p in pairs}]
    same = [i for i in sources if i in targets]
    left = zip([i for i in sources if i not in same], [i for i in targets if i not in same])
    return list(pairs) + [(i, i) for i in same] + list(left)


def place_tiles(wanted_late, tile_of, out_refs):
    me, space = lax.axis_index("snap"), lax.axis_index("space")
    snap_count = lax.axis_size("snap")
    chip_count, late = snap_count // 2, snap_count // 4
    band = chip_count + 1
    part_rows = out_refs[0].shape[1]

    def one(pair, slot):
        offset, k = pair // band, pair % band
        block = ((me // 2) ^ offset) * 2 + me % 2
        rel = ((block + k) % snap_count) ^ me
        is_late = jnp.logical_or(offset == late, rel // 2 == late)
        wanted = is_late if wanted_late else jnp.logical_not(is_late)

        @pl.when(wanted)
        def _():
            for n, out_ref in enumerate(out_refs):
                rows = pl.ds(pl.multiple_of((space ^ n) * part_rows, part_rows), part_rows)
                out_ref[slot] = tile_of(offset, rel, rows)

        return slot + jnp.where(wanted, 1, 0)

    lax.fori_loop(0, chip_count * band, one, 0)


def slot_count(snap_count, wanted_late):
    chip_count, late = snap_count // 2, snap_count // 4
    counts = []
    for me in range(snap_count):
        count = 0
        for offset in range(chip_count):
            block = ((me // 2) ^ offset) * 2 + me % 2
            for k in range(chip_count + 1):
                rel = ((block + k) % snap_count) ^ me
                count += (late in (offset, rel // 2)) == wanted_late
        counts.append(count)
    return max(counts)


def as_column(row):
    return jnp.transpose(jnp.broadcast_to(row, (LANES, LANES)))


def product(left, right):
    return lax.dot_general(left, right, (((1,), (0,)), ((), ())), preferred_element_type=jnp.float32)


def over_tiles(count, one_tile):
    group = math.gcd(count, 4)

    def some(step, carry):
        for n in range(group):
            one_tile(step * group + n)
        return carry

    lax.fori_loop(0, count // group, some, 0)


def split_kernel(hub_of, offsets, rows_ref, *refs):
    pieces, sems = refs[:-1], refs[-1]
    me = lax.axis_index("snap")
    copies = []
    for n, offset in enumerate(offsets):
        first = pl.multiple_of(hub_of(me ^ (2 * offset)), pieces[0].shape[0])
        copies.append(pltpu.make_async_copy(rows_ref.at[pl.ds(first, pieces[0].shape[0]), :], pieces[n], sems.at[n]))
    for copy in copies:
        copy.start()
    for copy in copies:
        copy.wait()


def sums_kernel(piece_ref, sums_ref):
    for tile in range(sums_ref.shape[0]):
        values = piece_ref[tile * LANES : (tile + 1) * LANES, :].astype(jnp.float32)
        sums_ref[tile : tile + 1, :] = jnp.sum(jnp.transpose(values), axis=0, keepdims=True)


def early_kernel(total_columns, near, late_same_ref, late_other_ref, *refs):
    blocks = refs[:near]
    turned_ref, mean_ref, spread_ref, *out_refs = refs[near:-2]
    fluct_ref, tiles_ref = refs[-2:]
    rows, width = blocks[0].shape

    def one_tile(tile):
        target = pl.ds(pl.multiple_of(tile * LANES, LANES), LANES)
        held = [ref[target, :].astype(jnp.float32) for ref in blocks]
        near_sum = jnp.sum(jnp.transpose(functools.reduce(jnp.add, held)), axis=0, keepdims=True)
        far_sum = late_same_ref[pl.ds(tile, 1), :] + late_other_ref[pl.ds(tile, 1), :]
        row = (near_sum + far_sum) * (1.0 / total_columns)
        mean_ref[pl.ds(tile, 1), :] = row
        mean = as_column(row)
        spread_ref[target, :] = mean
        for n in range(near):
            value = (held[n] - mean).astype(jnp.bfloat16)
            fluct_ref[target, n * width : (n + 1) * width] = value
            turned_ref[n * width : (n + 1) * width, target] = jnp.transpose(value)

    over_tiles(rows // LANES, one_tile)
    half = near // 2
    for first in range(0, near * width, 2 * width):
        columns = slice(first, min(first + 2 * width, near * width))
        tiles_ref[:, columns] = product(turned_ref[0 : half * width, :], fluct_ref[:, columns])
    late = lax.axis_size("snap") // 4

    def tile_of(offset, rel, rows):
        other = rel // 2
        row = offset - jnp.where(offset > late, 1, 0)
        column = other - jnp.where(other > late, 1, 0) + half * (rel % 2)
        rows = pl.ds(pl.multiple_of(row * width + rows.start, rows.size), rows.size)
        return tiles_ref[rows, pl.ds(pl.multiple_of(column * width, width), width)]

    place_tiles(False, tile_of, out_refs)


def late_kernel(near, spread_ref, same_ref, other_ref, turned_ref, *refs):
    out_refs, (fluct_ref, far_turned_ref, tiles_ref) = refs[:-3], refs[-3:]
    rows, width = same_ref.shape

    def one_tile(tile):
        target = pl.ds(pl.multiple_of(tile * LANES, LANES), LANES)
        mean = spread_ref[target, :]
        for n, ref in enumerate((same_ref, other_ref)):
            value = (ref[target, :].astype(jnp.float32) - mean).astype(jnp.bfloat16)
            fluct_ref[target, n * width : (n + 1) * width] = value
            far_turned_ref[n * width : (n + 1) * width, target] = jnp.transpose(value)

    over_tiles(rows // LANES, one_tile)
    half = near // 2
    step = half * width
    for first in range(0, near * width, step):
        with_far = product(turned_ref[first : first + step, :], fluct_ref[...])
        for n in range(half):
            place = first // width + n
            tile = with_far[n * width : (n + 1) * width, :]
            tiles_ref[place] = jnp.transpose(tile[:, :width])
            if first == 0:
                tiles_ref[near + 2 + 2 * n] = tile[:, :width]
                tiles_ref[near + 3 + 2 * n] = tile[:, width:]
    both = product(far_turned_ref[...], fluct_ref[...])
    tiles_ref[near] = both[:width, :width]
    tiles_ref[near + 1] = jnp.transpose(both[width:, :width])
    late = lax.axis_size("snap") // 4

    def tile_of(offset, rel, rows):
        other = rel // 2
        row = offset - jnp.where(offset > late, 1, 0)
        column = other - jnp.where(other > late, 1, 0) + half * (rel % 2)
        turned = jnp.where(other == late, near + rel % 2, column)
        place = jnp.where(offset == late, turned, near + 2 + 2 * row + rel % 2)
        return tiles_ref[place, rows, :]

    place_tiles(True, tile_of, out_refs)


def late_rounds(chip_count):
    snap_count = 2 * chip_count
    late = chip_count // 2
    wanted = []
    for chip in range(chip_count // 4, 3 * chip_count // 4):
        for offset in range(1, chip_count):
            counts = []
            for me in (2 * chip, 2 * chip + 1):
                block = ((me // 2) ^ offset) * 2 + me % 2
                rels = [((block + k) % snap_count) ^ me for k in range(chip_count + 1)]
                counts.append(sum(late in (offset, rel // 2) for rel in rels))
            if max(counts):
                wanted.append((-max(counts), chip, chip ^ offset))
    rounds = []
    for count, source, target in sorted(wanted):
        for pairs, _ in rounds:
            if source not in pairs and target not in pairs.values():
                pairs[source] = target
                break
        else:
            rounds.append(({source: target}, -count))
    return rounds


def is_far(chip, core, offset, k):
    snap_count = lax.axis_size("snap")
    late = snap_count // 4
    me = chip * 2 + core
    rel = (((chip ^ offset) * 2 + core + k) % snap_count) ^ me
    return jnp.logical_or(offset == late, rel // 2 == late)


def joined_near_kernel(space_count, mean_ref, *refs):
    firsts, out_refs = refs[:space_count], refs[space_count:]
    me = lax.axis_index("snap")
    _, part_rows, width = firsts[0].shape
    band = out_refs[0].shape[1] // width
    slot = 0
    for offset, out_ref in enumerate(out_refs):
        for k in range(band):
            far = is_far(me // 2, me % 2, offset, k)
            lanes = slice(k * width, (k + 1) * width)

            @pl.when(far)
            def _(out_ref=out_ref, lanes=lanes):
                out_ref[0:part_rows, lanes] = jnp.zeros((part_rows, width), jnp.float32)

            @pl.when(jnp.logical_not(far))
            def _(out_ref=out_ref, lanes=lanes, slot=slot):
                out_ref[0:part_rows, lanes] = functools.reduce(jnp.add, [ref[slot] for ref in firsts])

            slot = slot + jnp.where(far, 0, 1)
        for n in range(mean_ref.shape[0]):
            row = part_rows + n // band
            out_ref[row : row + 1, (n % band) * width : (n % band + 1) * width] = mean_ref[n : n + 1, :]


def joined_far_kernel(rounds, space_count, *refs):
    seconds, out_refs = refs[:space_count], refs[space_count:]
    me = lax.axis_index("snap")
    chip = me // 2
    _, _, width = seconds[0].shape
    chip_count = lax.axis_size("snap") // 2
    band = chip_count + 1
    slot = 0
    for offset in range(chip_count):
        here = [(0, chip_count)] if offset == 0 else []
        here += [(n + 1, source) for n, (pairs, _) in enumerate(rounds) for source in pairs if pairs[source] == source ^ offset]
        place = 0
        for k in range(band):
            far = is_far(chip, me % 2, offset, k)
            for n, source in here:
                mine = far if source == chip_count else jnp.logical_and(far, chip == source)

                @pl.when(mine)
                def _(n=n, slot=slot, place=place):
                    total = functools.reduce(jnp.add, [ref[slot] for ref in seconds])
                    lanes = pl.ds(pl.multiple_of(place * width, width), width)
                    out_refs[n][:, lanes] = total

            slot = slot + jnp.where(far, 1, 0)
            place = place + jnp.where(far, 1, 0)


def collected_kernel(first_chip, rounds, scale, *refs):
    me = lax.axis_index("snap")
    chip, core = me // 2, me % 2
    chip_count = lax.axis_size("snap") // 2
    hub_chips = chip_count // 2
    nears, fars, (gram_ref, mean_ref) = refs[:chip_count], refs[chip_count:-2], refs[-2:]
    part_rows, columns = gram_ref.shape
    total = jnp.zeros((part_rows, columns), jnp.float32)
    for offset, ref in enumerate(nears):
        hub = (chip ^ offset) - first_chip
        total = total + jnp.where((hub >= 0) & (hub < hub_chips), ref[0:part_rows, :], 0.0)
    gram_ref[...] = total * scale
    for n, ref in enumerate(fars):
        hub = chip - first_chip
        source = jnp.where((hub >= 0) & (hub < hub_chips), chip, -1)
        if n:
            source = -1
            for a, b in rounds[n - 1][0].items():
                source = jnp.where(chip == b, a, source)
        place = 0
        for k in range(columns // LANES):
            far = jnp.logical_and(source >= 0, is_far(source, core, source ^ chip, k))
            lanes = slice(k * LANES, (k + 1) * LANES)

            @pl.when(far)
            def _(ref=ref, lanes=lanes, place=place):
                sent = ref[:, pl.ds(pl.multiple_of(place * LANES, LANES), LANES)]
                gram_ref[:, lanes] = gram_ref[:, lanes] + sent * scale

            place = place + jnp.where(far, 1, 0)
    mean_rows = mean_ref.shape[0] // hub_chips
    band = columns // LANES
    for offset, ref in enumerate(nears):
        hub = (chip ^ offset) - first_chip

        @pl.when((hub >= 0) & (hub < hub_chips))
        def _(ref=ref, hub=hub):
            for n in range(mean_rows):
                row = part_rows + n // band
                mean_ref[pl.ds(hub * mean_rows + n, 1), :] = ref[row : row + 1, (n % band) * LANES : (n % band + 1) * LANES]


def per_device(snapshots):
    snap_count = lax.axis_size("snap")
    space_count = lax.axis_size("space")
    row_count, width = snapshots.shape
    chip_count = snap_count // 2
    first_chip, hub_chips = chip_count // 4, chip_count // 2
    hubs = list(range(2 * first_chip, 2 * (first_chip + hub_chips)))
    rows = row_count // hub_chips
    band = chip_count + 1
    part_rows = width // space_count
    late = chip_count // 2
    early = [offset for offset in range(chip_count) if offset != late]
    near = 2 * len(early)
    vmem = pl.BlockSpec(memory_space=pltpu.VMEM)

    def shaped(dtype, *shape):
        return jax.ShapeDtypeStruct(shape, dtype)

    def kernel(body, operands, out_shapes, scratch=(), flops=1000, raw=False):
        sizes = [int(np.prod(s.shape)) * jnp.dtype(s.dtype).itemsize for s in (*operands, *out_shapes)]
        sizes += [int(np.prod(s.shape)) * jnp.dtype(s.dtype).itemsize for s in scratch if hasattr(s, "shape") and s.memory_space == pltpu.VMEM]
        return pl.pallas_call(
            body,
            out_shape=list(out_shapes),
            in_specs=[pl.BlockSpec(memory_space=pltpu.HBM) if raw else vmem] * len(operands),
            out_specs=[vmem] * len(out_shapes),
            scratch_shapes=list(scratch),
            cost_estimate=pl.CostEstimate(flops=flops, bytes_accessed=0, transcendentals=0),
            compiler_params=pltpu.CompilerParams(vmem_limit_bytes=sum(sizes) + (6 << 20)),
        )(*operands)

    def hub_of(device):
        return jnp.clip(device // 2 - first_chip, 0, hub_chips - 1) * rows

    def to_hubs(x, offset, name):
        pairs = [(h ^ (2 * offset), h) for h in hubs]
        full = name == "sums" or offset != late
        return lax.ppermute(x, "snap", completed(pairs, snap_count) if full else pairs)

    def to_other_core(x):
        return lax.ppermute(x, "snap", [(i, i ^ 1) for i in range(snap_count)])

    piece = shaped(snapshots.dtype, rows, width)
    sums = shaped(jnp.float32, rows // LANES, LANES)
    offsets = early + [late]
    pieces = kernel(
        functools.partial(split_kernel, hub_of, offsets),
        [pltpu.with_memory_space_constraint(snapshots, pltpu.HBM)],
        [piece] * chip_count,
        [pltpu.SemaphoreType.DMA((chip_count,))],
        raw=True,
    )
    (far_sums,) = kernel(sums_kernel, [pieces[-1]], [sums])
    late_same = to_hubs(far_sums, late, "sums")
    blocks = {0: pieces[0]}
    for offset, x in zip(offsets[1:], pieces[1:]):
        blocks[offset] = to_hubs(x, offset, "bulk")
    late_other = to_other_core(late_same)
    passed = {offset: to_other_core(blocks[offset]) for offset in offsets}

    first_slots, second_slots = slot_count(snap_count, False), slot_count(snap_count, True)
    turned, mean_rows, spread, *first = kernel(
        functools.partial(early_kernel, width * snap_count, near),
        [late_same, late_other] + [blocks[offset] for offset in early] + [passed[offset] for offset in early],
        [shaped(jnp.bfloat16, near * width, rows), sums, shaped(jnp.float32, rows, LANES)]
        + [shaped(jnp.float32, first_slots, part_rows, width)] * space_count,
        [pltpu.VMEM((rows, near * width), jnp.bfloat16), pltpu.VMEM((near // 2 * width, near * width), jnp.float32)],
        flops=near * near * width * width * rows,
    )
    second = kernel(
        functools.partial(late_kernel, near),
        [spread, blocks[late], passed[late], turned],
        [shaped(jnp.float32, second_slots, part_rows, width)] * space_count,
        [
            pltpu.VMEM((rows, 2 * width), jnp.bfloat16),
            pltpu.VMEM((2 * width, rows), jnp.bfloat16),
            pltpu.VMEM((2 * near + 2, width, width), jnp.float32),
        ],
        flops=4 * snap_count * width * width * rows,
    )

    def over_space(parts):
        got = [parts[0]]
        for n in range(1, space_count):
            got.append(lax.ppermute(parts[n], "space", [(s, s ^ n) for s in range(space_count)]))
        return got

    mean_space = -(-(-(-(rows // LANES) // band)) // 8) * 8
    slab = shaped(jnp.float32, part_rows + mean_space, band * width)
    near_slabs = kernel(
        functools.partial(joined_near_kernel, space_count), [mean_rows, *over_space(first)], [slab] * chip_count
    )

    nears = [near_slabs[0]]
    for offset in range(1, chip_count):
        pairs = completed([(h, h ^ (2 * offset)) for h in hubs], snap_count)
        nears.append(lax.ppermute(near_slabs[offset], "snap", pairs))
    rounds = late_rounds(chip_count)
    far_slabs = kernel(
        functools.partial(joined_far_kernel, rounds, space_count),
        over_space(second),
        [shaped(jnp.float32, part_rows, count * width) for count in [band] + [count for _, count in rounds]],
    )
    fars = [far_slabs[0]]
    for n, (pairs, _) in enumerate(rounds):
        devices = [(2 * a + core, 2 * b + core) for a, b in pairs.items() for core in (0, 1)]
        fars.append(lax.ppermute(far_slabs[n + 1], "snap", completed(devices, snap_count)))
    gram_band, mean_field = kernel(
        functools.partial(collected_kernel, first_chip, rounds, 1.0 / (row_count * space_count)),
        nears + fars,
        [shaped(jnp.float32, part_rows, band * width), shaped(jnp.float32, row_count // LANES, LANES)],
    )
    return gram_band, mean_field.reshape(row_count)


def solution(mesh):
    return jax.shard_map(
        per_device,
        mesh=mesh,
        in_specs=(P("space", "snap"),),
        out_specs=(P(("snap", "space"), None), P("space")),
        check_vma=False,
    )
```

```python
import functools
import math

import jax
import jax.numpy as jnp
import numpy as np
from jax import lax
from jax.experimental import pallas as pl
from jax.experimental.pallas import tpu as pltpu
from jax.sharding import PartitionSpec as P


LANES = 128


def completed(pairs, count):
    sources = [i for i in range(count) if i not in {p[0] for p in pairs}]
    targets = [i for i in range(count) if i not in {p[1] for p in pairs}]
    same = [i for i in sources if i in targets]
    left = zip([i for i in sources if i not in same], [i for i in targets if i not in same])
    return list(pairs) + [(i, i) for i in same] + list(left)


def place_tiles(wanted_late, tile_of, out_refs):
    me, space = lax.axis_index("snap"), lax.axis_index("space")
    snap_count = lax.axis_size("snap")
    chip_count, late = snap_count // 2, snap_count // 4
    band = chip_count + 1
    part_rows = out_refs[0].shape[1]

    def one(pair, slot):
        offset, k = pair // band, pair % band
        block = ((me // 2) ^ offset) * 2 + me % 2
        rel = ((block + k) % snap_count) ^ me
        is_late = jnp.logical_or(offset == late, rel // 2 == late)
        wanted = is_late if wanted_late else jnp.logical_not(is_late)

        @pl.when(wanted)
        def _():
            for n, out_ref in enumerate(out_refs):
                rows = pl.ds(pl.multiple_of((space ^ n) * part_rows, part_rows), part_rows)
                out_ref[slot] = tile_of(offset, rel, rows)

        return slot + jnp.where(wanted, 1, 0)

    lax.fori_loop(0, chip_count * band, one, 0)


def slot_count(snap_count, wanted_late):
    chip_count, late = snap_count // 2, snap_count // 4
    counts = []
    for me in range(snap_count):
        count = 0
        for offset in range(chip_count):
            block = ((me // 2) ^ offset) * 2 + me % 2
            for k in range(chip_count + 1):
                rel = ((block + k) % snap_count) ^ me
                count += (late in (offset, rel // 2)) == wanted_late
        counts.append(count)
    return max(counts)


def as_column(row):
    return jnp.transpose(jnp.broadcast_to(row, (LANES, LANES)))


def product(left, right):
    return lax.dot_general(left, right, (((1,), (0,)), ((), ())), preferred_element_type=jnp.float32)


def over_tiles(count, one_tile):
    group = math.gcd(count, 4)

    def some(step, carry):
        for n in range(group):
            one_tile(step * group + n)
        return carry

    lax.fori_loop(0, count // group, some, 0)


def split_kernel(hub_of, offsets, rows_ref, *refs):
    pieces, sems = refs[:-1], refs[-1]
    me = lax.axis_index("snap")
    copies = []
    for n, offset in enumerate(offsets):
        first = pl.multiple_of(hub_of(me ^ (2 * offset)), pieces[0].shape[0])
        copies.append(pltpu.make_async_copy(rows_ref.at[pl.ds(first, pieces[0].shape[0]), :], pieces[n], sems.at[n]))
    for copy in copies:
        copy.start()
    for copy in copies:
        copy.wait()


def sums_kernel(piece_ref, sums_ref):
    for tile in range(sums_ref.shape[0]):
        values = piece_ref[tile * LANES : (tile + 1) * LANES, :].astype(jnp.float32)
        sums_ref[tile : tile + 1, :] = jnp.sum(jnp.transpose(values), axis=0, keepdims=True)


def early_kernel(total_columns, near, late_same_ref, late_other_ref, *refs):
    blocks = refs[:near]
    turned_ref, mean_ref, spread_ref, *out_refs = refs[near:-2]
    fluct_ref, tiles_ref = refs[-2:]
    rows, width = blocks[0].shape

    def one_tile(tile):
        target = pl.ds(pl.multiple_of(tile * LANES, LANES), LANES)
        held = [ref[target, :].astype(jnp.float32) for ref in blocks]
        near_sum = jnp.sum(jnp.transpose(functools.reduce(jnp.add, held)), axis=0, keepdims=True)
        far_sum = late_same_ref[pl.ds(tile, 1), :] + late_other_ref[pl.ds(tile, 1), :]
        row = (near_sum + far_sum) * (1.0 / total_columns)
        mean_ref[pl.ds(tile, 1), :] = row
        mean = as_column(row)
        spread_ref[target, :] = mean
        for n in range(near):
            value = (held[n] - mean).astype(jnp.bfloat16)
            fluct_ref[target, n * width : (n + 1) * width] = value
            turned_ref[n * width : (n + 1) * width, target] = jnp.transpose(value)

    over_tiles(rows // LANES, one_tile)
    half = near // 2
    for first in range(0, near * width, 2 * width):
        columns = slice(first, min(first + 2 * width, near * width))
        tiles_ref[:, columns] = product(turned_ref[0 : half * width, :], fluct_ref[:, columns])
    late = lax.axis_size("snap") // 4

    def tile_of(offset, rel, rows):
        other = rel // 2
        row = offset - jnp.where(offset > late, 1, 0)
        column = other - jnp.where(other > late, 1, 0) + half * (rel % 2)
        rows = pl.ds(pl.multiple_of(row * width + rows.start, rows.size), rows.size)
        return tiles_ref[rows, pl.ds(pl.multiple_of(column * width, width), width)]

    place_tiles(False, tile_of, out_refs)


def far_same_kernel(spread_ref, same_ref, turned_ref, far_turned_ref, tiles_ref, fluct_ref):
    rows, width = same_ref.shape
    near = turned_ref.shape[0] // width

    def one_tile(tile):
        target = pl.ds(pl.multiple_of(tile * LANES, LANES), LANES)
        value = (same_ref[target, :].astype(jnp.float32) - spread_ref[target, :]).astype(jnp.bfloat16)
        fluct_ref[target, :] = value
        far_turned_ref[:, target] = jnp.transpose(value)

    over_tiles(rows // LANES, one_tile)
    half = near // 2
    for first in range(0, near, half):
        column = product(turned_ref[first * width : (first + half) * width, :], fluct_ref[...])
        for n in range(half):
            tile = column[n * width : (n + 1) * width, :]
            tiles_ref[first + n] = jnp.transpose(tile)
            if first == 0:
                tiles_ref[near + 1 + n] = tile
    tiles_ref[near] = product(far_turned_ref[...], fluct_ref[...])


def far_other_kernel(near, spread_ref, other_ref, turned_ref, far_turned_ref, held_ref, *refs):
    out_refs, (fluct_ref, tiles_ref) = refs[:-2], refs[-2:]
    rows, width = other_ref.shape

    def one_tile(tile):
        target = pl.ds(pl.multiple_of(tile * LANES, LANES), LANES)
        fluct_ref[target, :] = (other_ref[target, :].astype(jnp.float32) - spread_ref[target, :]).astype(jnp.bfloat16)

    over_tiles(rows // LANES, one_tile)
    half = near // 2
    column = product(turned_ref[0 : half * width, :], fluct_ref[...])
    for n in range(half):
        tiles_ref[n] = column[n * width : (n + 1) * width, :]
    tiles_ref[half] = product(far_turned_ref[...], fluct_ref[...])
    late = lax.axis_size("snap") // 4

    def tile_of(offset, rel, rows):
        other, odd = rel // 2, rel % 2
        row = offset - jnp.where(offset > late, 1, 0)
        column = other - jnp.where(other > late, 1, 0) + half * odd
        place = jnp.where(offset == late, jnp.where(other == late, near, column), near + 1 + row)
        fresh = jnp.logical_and(other == late, odd == 1)
        place = jnp.where(fresh, 0, place)
        new = jnp.where(fresh, jnp.where(offset == late, half, row), 0)
        return jnp.where(fresh, tiles_ref[new, rows, :], held_ref[place, rows, :])

    place_tiles(True, tile_of, out_refs)


def late_rounds(chip_count):
    snap_count = 2 * chip_count
    late = chip_count // 2
    wanted = []
    for chip in range(chip_count // 4, 3 * chip_count // 4):
        for offset in range(1, chip_count):
            counts = []
            for me in (2 * chip, 2 * chip + 1):
                block = ((me // 2) ^ offset) * 2 + me % 2
                rels = [((block + k) % snap_count) ^ me for k in range(chip_count + 1)]
                counts.append(sum(late in (offset, rel // 2) for rel in rels))
            if max(counts):
                wanted.append((-max(counts), chip, chip ^ offset))
    rounds = []
    for count, source, target in sorted(wanted):
        for pairs, _ in rounds:
            if source not in pairs and target not in pairs.values():
                pairs[source] = target
                break
        else:
            rounds.append(({source: target}, -count))
    return rounds


def is_far(chip, core, offset, k):
    snap_count = lax.axis_size("snap")
    late = snap_count // 4
    me = chip * 2 + core
    rel = (((chip ^ offset) * 2 + core + k) % snap_count) ^ me
    return jnp.logical_or(offset == late, rel // 2 == late)


def joined_near_kernel(space_count, mean_ref, *refs):
    firsts, out_refs = refs[:space_count], refs[space_count:]
    me = lax.axis_index("snap")
    _, part_rows, width = firsts[0].shape
    band = out_refs[0].shape[1] // width
    chip_count = len(out_refs) + 1
    near_refs = dict(zip([offset for offset in range(chip_count) if offset != chip_count // 2], out_refs))
    slot = 0
    for offset, out_ref in near_refs.items():
        for k in range(band):
            far = is_far(me // 2, me % 2, offset, k)
            lanes = slice(k * width, (k + 1) * width)

            @pl.when(far)
            def _(out_ref=out_ref, lanes=lanes):
                out_ref[0:part_rows, lanes] = jnp.zeros((part_rows, width), jnp.float32)

            @pl.when(jnp.logical_not(far))
            def _(out_ref=out_ref, lanes=lanes, slot=slot):
                out_ref[0:part_rows, lanes] = functools.reduce(jnp.add, [ref[slot] for ref in firsts])

            slot = slot + jnp.where(far, 0, 1)
        put_means(mean_ref, out_ref, part_rows)


def put_means(mean_ref, out_ref, first_row):
    across = out_ref.shape[1] // LANES
    for n in range(mean_ref.shape[0]):
        lanes = slice((n % across) * LANES, (n % across + 1) * LANES)
        out_ref[first_row + n // across : first_row + n // across + 1, lanes] = mean_ref[n : n + 1, :]


def joined_far_kernel(rounds, space_count, mean_ref, *refs):
    seconds, out_refs = refs[:space_count], refs[space_count:]
    for out_ref in out_refs:
        if out_ref.shape[0] > seconds[0].shape[1]:
            put_means(mean_ref, out_ref, seconds[0].shape[1])
    me = lax.axis_index("snap")
    chip = me // 2
    _, part_rows, width = seconds[0].shape
    chip_count = lax.axis_size("snap") // 2
    band = chip_count + 1
    slot = 0
    for offset in range(chip_count):
        here = [(0, chip_count)] if offset == 0 else []
        here += [(n + 1, source) for n, (pairs, _) in enumerate(rounds) for source in pairs if pairs[source] == source ^ offset]
        place = 0
        for k in range(band):
            far = is_far(chip, me % 2, offset, k)
            for n, source in here:
                mine = far if source == chip_count else jnp.logical_and(far, chip == source)

                @pl.when(mine)
                def _(n=n, slot=slot, place=place):
                    total = functools.reduce(jnp.add, [ref[slot] for ref in seconds])
                    lanes = pl.ds(pl.multiple_of(place * width, width), width)
                    out_refs[n][0:part_rows, lanes] = total

            slot = slot + jnp.where(far, 1, 0)
            place = place + jnp.where(far, 1, 0)


def collected_kernel(first_chip, rounds, scale, *refs):
    me = lax.axis_index("snap")
    chip, core = me // 2, me % 2
    chip_count = lax.axis_size("snap") // 2
    hub_chips = chip_count // 2
    late = chip_count // 2
    nears, fars, (gram_ref, mean_ref) = refs[: chip_count - 1], refs[chip_count - 1 : -2], refs[-2:]
    nears = dict(zip([offset for offset in range(chip_count) if offset != late], nears))
    part_rows, columns = gram_ref.shape
    total = jnp.zeros((part_rows, columns), jnp.float32)
    for offset, ref in nears.items():
        hub = (chip ^ offset) - first_chip
        total = total + jnp.where((hub >= 0) & (hub < hub_chips), ref[0:part_rows, :], 0.0)
    gram_ref[...] = total * scale
    for n, ref in enumerate(fars):
        hub = chip - first_chip
        source = jnp.where((hub >= 0) & (hub < hub_chips), chip, -1)
        if n:
            source = -1
            for a, b in rounds[n - 1][0].items():
                source = jnp.where(chip == b, a, source)
        place = 0
        for k in range(columns // LANES):
            far = jnp.logical_and(source >= 0, is_far(source, core, source ^ chip, k))
            lanes = slice(k * LANES, (k + 1) * LANES)

            @pl.when(far)
            def _(ref=ref, lanes=lanes, place=place):
                sent = ref[0:part_rows, pl.ds(pl.multiple_of(place * LANES, LANES), LANES)]
                gram_ref[:, lanes] = gram_ref[:, lanes] + sent * scale

            place = place + jnp.where(far, 1, 0)
    mean_rows = mean_ref.shape[0] // hub_chips
    holders = nears | {late: next(ref for ref in fars if ref.shape[0] > part_rows)}
    for offset, ref in holders.items():
        hub = (chip ^ offset) - first_chip
        across = ref.shape[1] // LANES

        @pl.when((hub >= 0) & (hub < hub_chips))
        def _(ref=ref, hub=hub, across=across):
            for n in range(mean_rows):
                row, lanes = part_rows + n // across, slice((n % across) * LANES, (n % across + 1) * LANES)
                mean_ref[pl.ds(hub * mean_rows + n, 1), :] = ref[row : row + 1, lanes]


def per_device(snapshots):
    snap_count = lax.axis_size("snap")
    space_count = lax.axis_size("space")
    row_count, width = snapshots.shape
    chip_count = snap_count // 2
    first_chip, hub_chips = chip_count // 4, chip_count // 2
    hubs = list(range(2 * first_chip, 2 * (first_chip + hub_chips)))
    rows = row_count // hub_chips
    band = chip_count + 1
    part_rows = width // space_count
    late = chip_count // 2
    early = [offset for offset in range(chip_count) if offset != late]
    near = 2 * len(early)
    vmem = pl.BlockSpec(memory_space=pltpu.VMEM)

    def shaped(dtype, *shape):
        return jax.ShapeDtypeStruct(shape, dtype)

    def kernel(body, operands, out_shapes, scratch=(), flops=1000, raw=False):
        sizes = [int(np.prod(s.shape)) * jnp.dtype(s.dtype).itemsize for s in (*operands, *out_shapes)]
        sizes += [int(np.prod(s.shape)) * jnp.dtype(s.dtype).itemsize for s in scratch if hasattr(s, "shape") and s.memory_space == pltpu.VMEM]
        return pl.pallas_call(
            body,
            out_shape=list(out_shapes),
            in_specs=[pl.BlockSpec(memory_space=pltpu.HBM) if raw else vmem] * len(operands),
            out_specs=[vmem] * len(out_shapes),
            scratch_shapes=list(scratch),
            cost_estimate=pl.CostEstimate(flops=flops, bytes_accessed=0, transcendentals=0),
            compiler_params=pltpu.CompilerParams(vmem_limit_bytes=sum(sizes) + (6 << 20)),
        )(*operands)

    def hub_of(device):
        return jnp.clip(device // 2 - first_chip, 0, hub_chips - 1) * rows

    def to_hubs(x, offset, name):
        pairs = [(h ^ (2 * offset), h) for h in hubs]
        full = name == "sums" or offset != late
        return lax.ppermute(x, "snap", completed(pairs, snap_count) if full else pairs)

    def to_other_core(x):
        return lax.ppermute(x, "snap", [(i, i ^ 1) for i in range(snap_count)])

    piece = shaped(snapshots.dtype, rows, width)
    sums = shaped(jnp.float32, rows // LANES, LANES)
    offsets = early + [late]
    pieces = kernel(
        functools.partial(split_kernel, hub_of, offsets),
        [pltpu.with_memory_space_constraint(snapshots, pltpu.HBM)],
        [piece] * chip_count,
        [pltpu.SemaphoreType.DMA((chip_count,))],
        raw=True,
    )
    (far_sums,) = kernel(sums_kernel, [pieces[-1]], [sums])
    late_same = to_hubs(far_sums, late, "sums")
    blocks = {0: pieces[0]}
    for offset, x in zip(offsets[1:], pieces[1:]):
        blocks[offset] = to_hubs(x, offset, "bulk")
    late_other = to_other_core(late_same)
    passed = {offset: to_other_core(blocks[offset]) for offset in offsets}

    first_slots, second_slots = slot_count(snap_count, False), slot_count(snap_count, True)
    turned, mean_rows, spread, *first = kernel(
        functools.partial(early_kernel, width * snap_count, near),
        [late_same, late_other] + [blocks[offset] for offset in early] + [passed[offset] for offset in early],
        [shaped(jnp.bfloat16, near * width, rows), sums, shaped(jnp.float32, rows, LANES)]
        + [shaped(jnp.float32, first_slots, part_rows, width)] * space_count,
        [pltpu.VMEM((rows, near * width), jnp.bfloat16), pltpu.VMEM((near // 2 * width, near * width), jnp.float32)],
        flops=near * near * width * width * rows,
    )
    flops = 2 * snap_count * width * width * rows
    far_turned, held = kernel(
        far_same_kernel,
        [spread, blocks[late], turned],
        [shaped(jnp.bfloat16, width, rows), shaped(jnp.float32, near + near // 2 + 1, width, width)],
        [pltpu.VMEM((rows, width), jnp.bfloat16)],
        flops=flops,
    )
    second = kernel(
        functools.partial(far_other_kernel, near),
        [spread, passed[late], turned, far_turned, held],
        [shaped(jnp.float32, second_slots, part_rows, width)] * space_count,
        [pltpu.VMEM((rows, width), jnp.bfloat16), pltpu.VMEM((near // 2 + 1, width, width), jnp.float32)],
        flops=flops,
    )

    def over_space(parts):
        got = [parts[0]]
        for n in range(1, space_count):
            got.append(lax.ppermute(parts[n], "space", [(s, s ^ n) for s in range(space_count)]))
        return got

    mean_space = -(-(-(-(rows // LANES) // band)) // 8) * 8
    slab = shaped(jnp.float32, part_rows + mean_space, band * width)
    near_slabs = kernel(
        functools.partial(joined_near_kernel, space_count), [mean_rows, *over_space(first)], [slab] * len(early)
    )

    nears = [near_slabs[0]]
    for offset, x in zip(early[1:], near_slabs[1:]):
        pairs = completed([(h, h ^ (2 * offset)) for h in hubs], snap_count)
        nears.append(lax.ppermute(x, "snap", pairs))
    rounds = late_rounds(chip_count)

    def far_slab(pairs, count):
        below = -(-(-(-(rows // LANES) // count)) // 8) * 8 if any(a ^ b == late for a, b in pairs.items()) else 0
        return shaped(jnp.float32, part_rows + below, count * width)

    far_slabs = kernel(
        functools.partial(joined_far_kernel, rounds, space_count),
        [mean_rows, *over_space(second)],
        [shaped(jnp.float32, part_rows, band * width)] + [far_slab(*sent) for sent in rounds],
    )
    fars = [far_slabs[0]]
    for n, (pairs, _) in enumerate(rounds):
        devices = [(2 * a + core, 2 * b + core) for a, b in pairs.items() for core in (0, 1)]
        fars.append(lax.ppermute(far_slabs[n + 1], "snap", completed(devices, snap_count)))
    gram_band, mean_field = kernel(
        functools.partial(collected_kernel, first_chip, rounds, 1.0 / (row_count * space_count)),
        nears + fars,
        [shaped(jnp.float32, part_rows, band * width), shaped(jnp.float32, row_count // LANES, LANES)],
    )
    return gram_band, mean_field.reshape(row_count)


def solution(mesh):
    return jax.shard_map(
        per_device,
        mesh=mesh,
        in_specs=(P("space", "snap"),),
        out_specs=(P(("snap", "space"), None), P("space")),
        check_vma=False,
    )
```

```python
import functools
import math

import jax
import jax.numpy as jnp
import numpy as np
from jax import lax
from jax.experimental import pallas as pl
from jax.experimental.pallas import tpu as pltpu
from jax.sharding import PartitionSpec as P


LANES = 128


def completed(pairs, count):
    sources = [i for i in range(count) if i not in {p[0] for p in pairs}]
    targets = [i for i in range(count) if i not in {p[1] for p in pairs}]
    same = [i for i in sources if i in targets]
    left = zip([i for i in sources if i not in same], [i for i in targets if i not in same])
    return list(pairs) + [(i, i) for i in same] + list(left)


def tile_kind(chip, core, offset, k, snap_count):
    chip_count, late = snap_count // 2, snap_count // 4
    me = chip * 2 + core
    rel = (((chip ^ offset) * 2 + core + k) % snap_count) ^ me
    other = rel // 2
    is_hub = (chip >= chip_count // 4) & (chip < 3 * chip_count // 4)
    kept_other = (other != late) & (other != late ^ 1)
    kept_offset = (offset != late) & (offset != late ^ 1)
    near_hub = (offset != late) & (other != late)
    near_end = ((offset == 0) & (other <= 1)) | ((offset == 1) & (other == 0))
    far = is_hub & (((offset == late) & kept_other) | ((other == late) & kept_offset))
    return (is_hub & near_hub) | ((is_hub ^ True) & near_end), far, rel


def near_column(offset, late, count):
    return jnp.where(offset == late ^ 1, count - 1, offset - jnp.where(offset > late, 2, 0))


def place_tiles(wanted_far, tile_of, out_refs):
    me, space = lax.axis_index("snap"), lax.axis_index("space")
    snap_count = lax.axis_size("snap")
    chip_count = snap_count // 2
    band = chip_count + 1
    part_rows = out_refs[0].shape[1]

    def one(pair, slot):
        offset, k = pair // band, pair % band
        near, far, rel = tile_kind(me // 2, me % 2, offset, k, snap_count)
        wanted = far if wanted_far else near

        @pl.when(wanted)
        def _():
            for n, out_ref in enumerate(out_refs):
                rows = pl.ds(pl.multiple_of((space ^ n) * part_rows, part_rows), part_rows)
                out_ref[slot] = tile_of(offset, rel, rows)

        return slot + jnp.where(wanted, 1, 0)

    lax.fori_loop(0, chip_count * band, one, 0)


def slot_count(snap_count, wanted_far):
    chip_count = snap_count // 2
    pairs = [(offset, k) for offset in range(chip_count) for k in range(chip_count + 1)]
    devices = [(chip, core) for chip in range(chip_count) for core in (0, 1)]
    return max(sum(tile_kind(*device, *pair, snap_count)[int(wanted_far)] for pair in pairs) for device in devices)


def as_column(row):
    return jnp.transpose(jnp.broadcast_to(row, (LANES, LANES)))


def product(left, right):
    return lax.dot_general(left, right, (((1,), (0,)), ((), ())), preferred_element_type=jnp.float32)


def over_tiles(count, one_tile):
    group = math.gcd(count, 4)

    def some(step, carry):
        for n in range(group):
            one_tile(step * group + n)
        return carry

    lax.fori_loop(0, count // group, some, 0)


def split_kernel(hub_of, offsets, rows_ref, *refs):
    pieces, sems = refs[:-1], refs[-1]
    me = lax.axis_index("snap")
    copies = []
    for n, offset in enumerate(offsets):
        first = pl.multiple_of(hub_of(me ^ (2 * offset)), pieces[0].shape[0])
        copies.append(pltpu.make_async_copy(rows_ref.at[pl.ds(first, pieces[0].shape[0]), :], pieces[n], sems.at[n]))
    for copy in copies:
        copy.start()
    for copy in copies:
        copy.wait()


def sums_kernel(*refs):
    pieces, sums_ref = refs[:-1], refs[-1]
    count = pieces[0].shape[0] // LANES
    for n, piece_ref in enumerate(pieces):
        for tile in range(count):
            values = piece_ref[tile * LANES : (tile + 1) * LANES, :].astype(jnp.float32)
            row = n * count + tile
            sums_ref[row : row + 1, :] = jnp.sum(jnp.transpose(values), axis=0, keepdims=True)


def chip_sums_kernel(own_ref, mate_ref, *out_refs):
    count = out_refs[0].shape[0]
    for n, out_ref in enumerate(out_refs):
        rows = slice(n * count, (n + 1) * count)
        out_ref[...] = own_ref[rows, :] + mate_ref[rows, :]


def early_kernel(total_columns, near, late_sums_ref, *refs):
    half = near // 2
    rest_sums, blocks = refs[: half - 2], refs[half - 2 : half - 2 + near]
    turned_ref, mean_ref, spread_ref, *out_refs = refs[half - 2 + near : -2]
    fluct_ref, tiles_ref = refs[-2:]
    rows, width = blocks[0].shape
    late = lax.axis_size("snap") // 4
    chip = lax.axis_index("snap") // 2
    is_hub = (chip >= late // 2) & (chip < late // 2 + late)

    def one_tile(tile):
        target = pl.ds(pl.multiple_of(tile * LANES, LANES), LANES)
        held = [ref[target, :].astype(jnp.float32) for ref in blocks]
        always = functools.reduce(jnp.add, [held[n] for n in range(near) if n % half < 2])
        at_hubs = functools.reduce(jnp.add, [held[n] for n in range(near) if n % half >= 2])
        near_sum = jnp.sum(jnp.transpose(always + jnp.where(is_hub, at_hubs, 0.0)), axis=0, keepdims=True)
        rest = functools.reduce(jnp.add, [ref[pl.ds(tile, 1), :] for ref in rest_sums])
        far_sum = late_sums_ref[pl.ds(tile, 1), :] + jnp.where(is_hub, 0.0, rest)
        row = (near_sum + far_sum) * (1.0 / total_columns)
        mean_ref[pl.ds(tile, 1), :] = row
        mean = as_column(row)
        spread_ref[target, :] = mean
        for n in range(near):
            value = (held[n] - mean).astype(jnp.bfloat16)
            fluct_ref[target, n * width : (n + 1) * width] = value
            if n < near - 1:
                turned_ref[n * width : (n + 1) * width, target] = jnp.transpose(value)

    over_tiles(rows // LANES, one_tile)
    for first in range(0, near * width, 2 * width):
        columns = slice(first, min(first + 2 * width, near * width))
        tiles_ref[:, columns] = product(turned_ref[0 : half * width, :], fluct_ref[:, columns])

    def tile_of(offset, rel, rows):
        row = near_column(offset, late, half)
        column = near_column(rel // 2, late, half) + half * (rel % 2)
        rows = pl.ds(pl.multiple_of(row * width + rows.start, rows.size), rows.size)
        return tiles_ref[rows, pl.ds(pl.multiple_of(column * width, width), width)]

    place_tiles(False, tile_of, out_refs)


def far_same_kernel(half, spread_ref, same_ref, turned_ref, tiles_ref, fluct_ref):
    rows, width = same_ref.shape

    def one_tile(tile):
        target = pl.ds(pl.multiple_of(tile * LANES, LANES), LANES)
        fluct_ref[target, :] = (same_ref[target, :].astype(jnp.float32) - spread_ref[target, :]).astype(jnp.bfloat16)

    over_tiles(rows // LANES, one_tile)
    kept = half - 1
    for odd in (0, 1):
        first = odd * half * width
        column = product(turned_ref[first : first + kept * width, :], fluct_ref[...])
        for n in range(kept):
            tile = column[n * width : (n + 1) * width, :]
            tiles_ref[odd * kept + n] = jnp.transpose(tile)
            if not odd:
                tiles_ref[2 * kept + n] = tile


def far_other_kernel(half, spread_ref, other_ref, turned_ref, held_ref, *refs):
    out_refs, (fluct_ref, tiles_ref) = refs[:-2], refs[-2:]
    rows, width = other_ref.shape

    def one_tile(tile):
        target = pl.ds(pl.multiple_of(tile * LANES, LANES), LANES)
        fluct_ref[target, :] = (other_ref[target, :].astype(jnp.float32) - spread_ref[target, :]).astype(jnp.bfloat16)

    over_tiles(rows // LANES, one_tile)
    kept = half - 1
    column = product(turned_ref[0 : kept * width, :], fluct_ref[...])
    for n in range(kept):
        tiles_ref[n] = column[n * width : (n + 1) * width, :]
    late = lax.axis_size("snap") // 4

    def tile_of(offset, rel, rows):
        other, odd = rel // 2, rel % 2
        row = near_column(offset, late, half)
        mirrored = near_column(other, late, half) + kept * odd
        fresh = (other == late) & (odd == 1)
        place = jnp.where(fresh, 0, jnp.where(offset == late, mirrored, 2 * kept + row))
        return jnp.where(fresh, tiles_ref[jnp.where(fresh, row, 0), rows, :], held_ref[place, rows, :])

    place_tiles(True, tile_of, out_refs)


def far_rounds(chip_count):
    wanted = []
    for chip in range(chip_count // 4, 3 * chip_count // 4):
        for offset in range(1, chip_count):
            kinds = [[tile_kind(chip, core, offset, k, 2 * chip_count)[1] for k in range(chip_count + 1)] for core in (0, 1)]
            count = max(sum(kind) for kind in kinds)
            if count:
                wanted.append((-count, chip, chip ^ offset))
    rounds = []
    for count, source, target in sorted(wanted):
        for pairs, _ in rounds:
            if source not in pairs and target not in pairs.values():
                pairs[source] = target
                break
        else:
            rounds.append(({source: target}, -count))
    return rounds


def joined_near_kernel(space_count, mean_ref, *refs):
    firsts, out_refs = refs[:space_count], refs[space_count:]
    me = lax.axis_index("snap")
    _, part_rows, width = firsts[0].shape
    band = out_refs[0].shape[1] // width
    chip_count = len(out_refs) + 1
    near_refs = dict(zip([offset for offset in range(chip_count) if offset != chip_count // 2], out_refs))
    slot = 0
    for offset, out_ref in near_refs.items():
        for k in range(band):
            near = tile_kind(me // 2, me % 2, offset, k, lax.axis_size("snap"))[0]
            lanes = slice(k * width, (k + 1) * width)

            @pl.when(jnp.logical_not(near))
            def _(out_ref=out_ref, lanes=lanes):
                out_ref[0:part_rows, lanes] = jnp.zeros((part_rows, width), jnp.float32)

            @pl.when(near)
            def _(out_ref=out_ref, lanes=lanes, slot=slot):
                out_ref[0:part_rows, lanes] = functools.reduce(jnp.add, [ref[slot] for ref in firsts])

            slot = slot + jnp.where(near, 1, 0)
        put_means(mean_ref, out_ref, part_rows)


def put_means(mean_ref, out_ref, first_row):
    across = out_ref.shape[1] // LANES
    for n in range(mean_ref.shape[0]):
        lanes = slice((n % across) * LANES, (n % across + 1) * LANES)
        out_ref[first_row + n // across : first_row + n // across + 1, lanes] = mean_ref[n : n + 1, :]


def joined_far_kernel(rounds, space_count, *refs):
    seconds, out_refs = refs[:space_count], refs[space_count:]
    me = lax.axis_index("snap")
    chip = me // 2
    _, _, width = seconds[0].shape
    chip_count = lax.axis_size("snap") // 2
    band = chip_count + 1
    slot = 0
    for offset in range(chip_count):
        here = [(0, chip_count)] if offset == 0 else []
        here += [(n + 1, source) for n, (pairs, _) in enumerate(rounds) for source in pairs if pairs[source] == source ^ offset]
        place = 0
        for k in range(band):
            far = tile_kind(chip, me % 2, offset, k, 2 * chip_count)[1]
            for n, source in here:
                mine = far if source == chip_count else jnp.logical_and(far, chip == source)

                @pl.when(mine)
                def _(n=n, slot=slot, place=place):
                    total = functools.reduce(jnp.add, [ref[slot] for ref in seconds])
                    lanes = pl.ds(pl.multiple_of(place * width, width), width)
                    out_refs[n][:, lanes] = total

            slot = slot + jnp.where(far, 1, 0)
            place = place + jnp.where(far, 1, 0)


def collected_kernel(first_chip, rounds, scale, *refs):
    me = lax.axis_index("snap")
    chip, core = me // 2, me % 2
    chip_count = lax.axis_size("snap") // 2
    hub_chips = chip_count // 2
    late = chip_count // 2
    nears, fars, (gram_ref, mean_ref) = refs[: chip_count - 1], refs[chip_count - 1 : -2], refs[-2:]
    nears = dict(zip([offset for offset in range(chip_count) if offset != late], nears))
    part_rows, columns = gram_ref.shape
    is_hub = (chip >= first_chip) & (chip < first_chip + hub_chips)
    total = jnp.zeros((part_rows, columns), jnp.float32)
    for offset, ref in nears.items():
        hub = (chip ^ offset) - first_chip
        held = True if offset < 2 else (hub >= 0) & (hub < hub_chips)
        total = total + jnp.where(held, ref[0:part_rows, :], 0.0)
    gram_ref[...] = total * scale
    for n, ref in enumerate(fars):
        source = jnp.where(is_hub, chip, -1)
        if n:
            source = -1
            for a, b in rounds[n - 1][0].items():
                source = jnp.where(chip == b, a, source)
        place = 0
        for k in range(columns // LANES):
            far = jnp.logical_and(source >= 0, tile_kind(source, core, source ^ chip, k, 2 * chip_count)[1])
            lanes = slice(k * LANES, (k + 1) * LANES)

            @pl.when(far)
            def _(ref=ref, lanes=lanes, place=place):
                sent = ref[:, pl.ds(pl.multiple_of(place * LANES, LANES), LANES)]
                gram_ref[:, lanes] = gram_ref[:, lanes] + sent * scale

            place = place + jnp.where(far, 1, 0)
    mean_rows = mean_ref.shape[0] // hub_chips
    across = columns // LANES
    for offset, ref in nears.items():
        hub = (chip ^ offset) - first_chip
        if offset == 0:
            hub = jnp.where(is_hub, hub, (chip ^ late) - first_chip)

        @pl.when((hub >= 0) & (hub < hub_chips))
        def _(ref=ref, hub=hub):
            for n in range(mean_rows):
                row, lanes = part_rows + n // across, slice((n % across) * LANES, (n % across + 1) * LANES)
                mean_ref[pl.ds(hub * mean_rows + n, 1), :] = ref[row : row + 1, lanes]


def per_device(snapshots):
    snap_count = lax.axis_size("snap")
    space_count = lax.axis_size("space")
    row_count, width = snapshots.shape
    chip_count = snap_count // 2
    first_chip, hub_chips = chip_count // 4, chip_count // 2
    hubs = list(range(2 * first_chip, 2 * (first_chip + hub_chips)))
    rows = row_count // hub_chips
    band = chip_count + 1
    part_rows = width // space_count
    late = chip_count // 2
    early = [offset for offset in range(chip_count) if offset not in (late, late ^ 1)] + [late ^ 1]
    near = 2 * len(early)
    vmem = pl.BlockSpec(memory_space=pltpu.VMEM)

    def shaped(dtype, *shape):
        return jax.ShapeDtypeStruct(shape, dtype)

    def kernel(body, operands, out_shapes, scratch=(), flops=1000, raw=False):
        sizes = [int(np.prod(s.shape)) * jnp.dtype(s.dtype).itemsize for s in (*operands, *out_shapes)]
        sizes += [int(np.prod(s.shape)) * jnp.dtype(s.dtype).itemsize for s in scratch if hasattr(s, "shape") and s.memory_space == pltpu.VMEM]
        return pl.pallas_call(
            body,
            out_shape=list(out_shapes),
            in_specs=[pl.BlockSpec(memory_space=pltpu.HBM) if raw else vmem] * len(operands),
            out_specs=[vmem] * len(out_shapes),
            scratch_shapes=list(scratch),
            cost_estimate=pl.CostEstimate(flops=flops, bytes_accessed=0, transcendentals=0),
            compiler_params=pltpu.CompilerParams(vmem_limit_bytes=sum(sizes) + (6 << 20)),
        )(*operands)

    def hub_of(device):
        chip = device // 2
        is_hub = (chip >= first_chip) & (chip < first_chip + hub_chips)
        return (jnp.where(is_hub, chip, chip ^ late) - first_chip) * rows

    def to_hubs(x, offset, name):
        pairs = [(h ^ (2 * offset), h) for h in hubs]
        if name == "sums" or offset == 1:
            pairs = [(i ^ (2 * offset), i) for i in range(snap_count)]
        elif offset != late:
            pairs = completed(pairs, snap_count)
        return lax.ppermute(x, "snap", pairs)

    def to_other_core(x):
        return lax.ppermute(x, "snap", [(i, i ^ 1) for i in range(snap_count)])

    piece = shaped(snapshots.dtype, rows, width)
    sums = shaped(jnp.float32, rows // LANES, LANES)
    offsets = early + [late]
    pieces = kernel(
        functools.partial(split_kernel, hub_of, offsets),
        [pltpu.with_memory_space_constraint(snapshots, pltpu.HBM)],
        [piece] * chip_count,
        [pltpu.SemaphoreType.DMA((chip_count,))],
        raw=True,
    )
    summed = [late] + early[2:]
    by_offset = dict(zip(offsets, pieces))
    (far_sums,) = kernel(
        sums_kernel,
        [by_offset[offset] for offset in summed],
        [shaped(jnp.float32, len(summed) * (rows // LANES), LANES)],
    )
    blocks = {0: pieces[0]}
    for offset, x in zip(offsets[1:], pieces[1:]):
        blocks[offset] = to_hubs(x, offset, "bulk")
    chip_sums = kernel(chip_sums_kernel, [far_sums, to_other_core(far_sums)], [sums] * len(summed))
    came = {offset: to_hubs(x, offset, "sums") for offset, x in zip(summed, chip_sums)}
    passed = {offset: to_other_core(blocks[offset]) for offset in offsets}

    first_slots, second_slots = slot_count(snap_count, False), slot_count(snap_count, True)
    half, kept = len(early), len(early) - 1
    turned, mean_rows, spread, *first = kernel(
        functools.partial(early_kernel, width * snap_count, near),
        [came[offset] for offset in summed] + [blocks[offset] for offset in early] + [passed[offset] for offset in early],
        [shaped(jnp.bfloat16, (near - 1) * width, rows), sums, shaped(jnp.float32, rows, LANES)]
        + [shaped(jnp.float32, first_slots, part_rows, width)] * space_count,
        [pltpu.VMEM((rows, near * width), jnp.bfloat16), pltpu.VMEM((half * width, near * width), jnp.float32)],
        flops=near * near * width * width * rows,
    )
    flops = 2 * snap_count * width * width * rows
    (held,) = kernel(
        functools.partial(far_same_kernel, half),
        [spread, blocks[late], turned],
        [shaped(jnp.float32, 3 * kept, width, width)],
        [pltpu.VMEM((rows, width), jnp.bfloat16)],
        flops=flops,
    )
    second = kernel(
        functools.partial(far_other_kernel, half),
        [spread, passed[late], turned, held],
        [shaped(jnp.float32, second_slots, part_rows, width)] * space_count,
        [pltpu.VMEM((rows, width), jnp.bfloat16), pltpu.VMEM((kept, width, width), jnp.float32)],
        flops=flops,
    )

    def over_space(parts):
        got = [parts[0]]
        for n in range(1, space_count):
            got.append(lax.ppermute(parts[n], "space", [(s, s ^ n) for s in range(space_count)]))
        return got

    mean_space = -(-(-(-(rows // LANES) // band)) // 8) * 8
    slab = shaped(jnp.float32, part_rows + mean_space, band * width)
    near_slabs = kernel(
        functools.partial(joined_near_kernel, space_count), [mean_rows, *over_space(first)], [slab] * len(early)
    )

    nears = [near_slabs[0]]
    for offset, x in zip(early[1:], near_slabs[1:]):
        sources = range(snap_count) if offset == 1 else hubs
        pairs = completed([(i, i ^ (2 * offset)) for i in sources], snap_count)
        nears.append(lax.ppermute(x, "snap", pairs))
    rounds = far_rounds(chip_count)
    far_slabs = kernel(
        functools.partial(joined_far_kernel, rounds, space_count),
        over_space(second),
        [shaped(jnp.float32, part_rows, count * width) for count in [band] + [count for _, count in rounds]],
    )
    fars = [far_slabs[0]]
    for n, (pairs, _) in enumerate(rounds):
        devices = [(2 * a + core, 2 * b + core) for a, b in pairs.items() for core in (0, 1)]
        fars.append(lax.ppermute(far_slabs[n + 1], "snap", completed(devices, snap_count)))
    gram_band, mean_field = kernel(
        functools.partial(collected_kernel, first_chip, rounds, 1.0 / (row_count * space_count)),
        nears + fars,
        [shaped(jnp.float32, part_rows, band * width), shaped(jnp.float32, row_count // LANES, LANES)],
    )
    return gram_band, mean_field.reshape(row_count)


def solution(mesh):
    return jax.shard_map(
        per_device,
        mesh=mesh,
        in_specs=(P("space", "snap"),),
        out_specs=(P(("snap", "space"), None), P("space")),
        check_vma=False,
    )
```

```python
import functools
import math

import jax
import jax.numpy as jnp
import numpy as np
from jax import lax
from jax.experimental import pallas as pl
from jax.experimental.pallas import tpu as pltpu
from jax.sharding import PartitionSpec as P


LANES = 128
CHUNKS = 4
UNROLLED = 32


def completed(pairs, count):
    sources = [i for i in range(count) if i not in {p[0] for p in pairs}]
    targets = [i for i in range(count) if i not in {p[1] for p in pairs}]
    same = [i for i in sources if i in targets]
    left = zip([i for i in sources if i not in same], [i for i in targets if i not in same])
    return list(pairs) + [(i, i) for i in same] + list(left)


def tile_kind(chip, core, offset, k, snap_count):
    chip_count, late = snap_count // 2, snap_count // 4
    me = chip * 2 + core
    rel = (((chip ^ offset) * 2 + core + k) % snap_count) ^ me
    other = rel // 2
    is_hub = (chip >= chip_count // 4) & (chip < 3 * chip_count // 4)
    kept_other = (other != late) & (other != late ^ 1)
    kept_offset = (offset != late) & (offset != late ^ 1)
    near_hub = (offset != late) & (other != late)
    near_end = ((offset == 0) & (other <= 1)) | ((offset == 1) & (other == 0))
    far = is_hub & (((offset == late) & kept_other) | ((other == late) & kept_offset))
    return (is_hub & near_hub) | ((is_hub ^ True) & near_end), far, rel


def near_column(offset, late, count):
    return jnp.where(offset == late ^ 1, count - 1, offset - jnp.where(offset > late, 2, 0))


def other_column(offset, late, count):
    column = near_column(offset, late, count)
    return jnp.where(offset == 1, count - 1, column - jnp.where(column > 1, 1, 0))


def place_tiles(wanted_far, tile_of, out_refs):
    me, space = lax.axis_index("snap"), lax.axis_index("space")
    snap_count = lax.axis_size("snap")
    chip_count = snap_count // 2
    band = chip_count + 1
    part_rows = out_refs[0].shape[1]

    def one(pair, slot):
        offset, k = pair // band, pair % band
        near, far, rel = tile_kind(me // 2, me % 2, offset, k, snap_count)
        wanted = far if wanted_far else near

        @pl.when(wanted)
        def _():
            for n, out_ref in enumerate(out_refs):
                rows = pl.ds(pl.multiple_of((space ^ n) * part_rows, part_rows), part_rows)
                out_ref[slot] = tile_of(offset, rel, rows)

        return slot + jnp.where(wanted, 1, 0)

    if chip_count * band > UNROLLED:
        lax.fori_loop(0, chip_count * band, one, 0)
        return
    slot = 0
    for pair in range(chip_count * band):
        slot = one(pair, slot)


def slot_count(snap_count, wanted_far):
    chip_count = snap_count // 2
    pairs = [(offset, k) for offset in range(chip_count) for k in range(chip_count + 1)]
    devices = [(chip, core) for chip in range(chip_count) for core in (0, 1)]
    return max(sum(tile_kind(*device, *pair, snap_count)[int(wanted_far)] for pair in pairs) for device in devices)


def as_column(row):
    return jnp.transpose(jnp.broadcast_to(row, (LANES, LANES)))


def product(left, right):
    return lax.dot_general(left, right, (((1,), (0,)), ((), ())), preferred_element_type=jnp.float32)


def over_tiles(count, one_tile):
    for tile in range(count):
        one_tile(tile)


def split_kernel(hub_of, rows_ref, own_ref, next_ref, sems):
    me = lax.axis_index("snap")
    copies = []
    for n, (device, piece_ref) in enumerate(((me, own_ref), (me ^ 2, next_ref))):
        first = pl.multiple_of(hub_of(device), piece_ref.shape[0])
        copies.append(pltpu.make_async_copy(rows_ref.at[pl.ds(first, piece_ref.shape[0]), :], piece_ref, sems.at[n]))
    for copy in copies:
        copy.start()
    for copy in copies:
        copy.wait()


def sums_kernel(*refs):
    pieces, sums_ref = refs[:-1], refs[-1]
    count = pieces[0].shape[0] // LANES
    for n, piece_ref in enumerate(pieces):
        for tile in range(count):
            values = piece_ref[tile * LANES : (tile + 1) * LANES, :].astype(jnp.float32)
            row = n * count + tile
            sums_ref[row : row + 1, :] = jnp.sum(jnp.transpose(values), axis=0, keepdims=True)


def chip_sums_kernel(own_ref, mate_ref, *out_refs):
    count = out_refs[0].shape[0]
    for n, out_ref in enumerate(out_refs):
        rows = slice(n * count, (n + 1) * count)
        out_ref[...] = own_ref[rows, :] + mate_ref[rows, :]


def near_kernel(total_columns, half, chunks, *refs):
    sums_refs, blocks = refs[: half + 1], refs[half + 1 : 3 * half]
    turned_ref, mean_ref, spread_ref, tiles_ref, fluct_ref = refs[3 * half :]
    rows, width = blocks[0].shape
    step = rows // chunks
    for chunk in range(chunks):
        for tile in range(chunk * step // LANES, (chunk + 1) * step // LANES):
            target = slice(tile * LANES, (tile + 1) * LANES)
            total = functools.reduce(jnp.add, [ref[tile : tile + 1, :] for ref in sums_refs])
            row = total * (1.0 / total_columns)
            mean_ref[tile : tile + 1, :] = row
            mean = as_column(row)
            spread_ref[target, :] = mean
            for n, ref in enumerate(blocks):
                value = (ref[target, :].astype(jnp.float32) - mean).astype(jnp.bfloat16)
                fluct_ref[target, n * width : (n + 1) * width] = value
                if n < len(blocks) - 1:
                    turned_ref[n * width : (n + 1) * width, target] = jnp.transpose(value)
        across = slice(chunk * step, (chunk + 1) * step)
        left = turned_ref[0 : half * width, across]
        for first in range(0, len(blocks) * width, 2 * width):
            columns = slice(first, min(first + 2 * width, len(blocks) * width))
            part = product(left, fluct_ref[across, columns])
            tiles_ref[:, columns] = part if chunk == 0 else tiles_ref[:, columns] + part


def near_last_kernel(half, spread_ref, last_ref, turned_ref, held_ref, last_turned_ref, *refs):
    out_refs, (fluct_ref, tiles_ref) = refs[:-2], refs[-2:]
    rows, width = last_ref.shape
    late = lax.axis_size("snap") // 4

    def one_tile(tile):
        target = slice(tile * LANES, (tile + 1) * LANES)
        value = (last_ref[target, :].astype(jnp.float32) - spread_ref[target, :]).astype(jnp.bfloat16)
        fluct_ref[target, :] = value
        last_turned_ref[:, target] = jnp.transpose(value)

    over_tiles(rows // LANES, one_tile)
    tiles_ref[...] = product(turned_ref[0 : half * width, :], fluct_ref[...])

    def tile_of(offset, rel, rows):
        row = near_column(offset, late, half)
        other = rel // 2
        odd = rel % 2 == 1
        column = jnp.where(odd, half + other_column(other, late, half), near_column(other, late, half))
        last = column == 2 * half - 1
        rows = pl.ds(pl.multiple_of(row * width + rows.start, rows.size), rows.size)
        lanes = pl.ds(pl.multiple_of(jnp.where(last, 0, column) * width, width), width)
        return jnp.where(last, tiles_ref[rows, :], held_ref[rows, lanes])

    place_tiles(False, tile_of, out_refs)


def far_same_kernel(half, spread_ref, same_ref, turned_ref, last_turned_ref, tiles_ref, fluct_ref):
    rows, width = same_ref.shape

    def one_tile(tile):
        target = slice(tile * LANES, (tile + 1) * LANES)
        fluct_ref[target, :] = (same_ref[target, :].astype(jnp.float32) - spread_ref[target, :]).astype(jnp.bfloat16)

    over_tiles(rows // LANES, one_tile)
    kept = half - 1
    own = product(turned_ref[0 : kept * width, :], fluct_ref[...])
    other = product(turned_ref[half * width : (half + kept - 1) * width, :], fluct_ref[...])
    last = product(last_turned_ref[...], fluct_ref[...])
    for n in range(kept):
        tile = own[n * width : (n + 1) * width, :]
        tiles_ref[n] = jnp.transpose(tile)
        tiles_ref[2 * kept + n] = tile
    for n in range(kept - 1):
        tiles_ref[kept + n] = jnp.transpose(other[n * width : (n + 1) * width, :])
    tiles_ref[2 * kept - 1] = jnp.transpose(last)


def far_other_kernel(half, spread_ref, other_ref, turned_ref, held_ref, *refs):
    out_refs, (fluct_ref, tiles_ref) = refs[:-2], refs[-2:]
    rows, width = other_ref.shape

    def one_tile(tile):
        target = slice(tile * LANES, (tile + 1) * LANES)
        fluct_ref[target, :] = (other_ref[target, :].astype(jnp.float32) - spread_ref[target, :]).astype(jnp.bfloat16)

    over_tiles(rows // LANES, one_tile)
    kept = half - 1
    column = product(turned_ref[0 : kept * width, :], fluct_ref[...])
    for n in range(kept):
        tiles_ref[n] = column[n * width : (n + 1) * width, :]
    late = lax.axis_size("snap") // 4

    def tile_of(offset, rel, rows):
        other, odd = rel // 2, rel % 2
        row = near_column(offset, late, half)
        beyond = other_column(other, late, half)
        beyond = kept + jnp.where(other == 1, kept - 1, beyond)
        mirrored = jnp.where(odd == 1, beyond, near_column(other, late, half))
        fresh = (other == late) & (odd == 1)
        place = jnp.where(fresh, 0, jnp.where(offset == late, mirrored, 2 * kept + row))
        return jnp.where(fresh, tiles_ref[jnp.where(fresh, row, 0), rows, :], held_ref[place, rows, :])

    place_tiles(True, tile_of, out_refs)


def far_rounds(chip_count):
    wanted = []
    for chip in range(chip_count // 4, 3 * chip_count // 4):
        for offset in range(1, chip_count):
            kinds = [[tile_kind(chip, core, offset, k, 2 * chip_count)[1] for k in range(chip_count + 1)] for core in (0, 1)]
            count = max(sum(kind) for kind in kinds)
            if count:
                wanted.append((-count, chip, chip ^ offset))
    rounds = []
    for count, source, target in sorted(wanted):
        for pairs, _ in rounds:
            if source not in pairs and target not in pairs.values():
                pairs[source] = target
                break
        else:
            rounds.append(({source: target}, -count))
    return rounds


def joined_near_kernel(space_count, mean_ref, *refs):
    firsts, out_refs = refs[:space_count], refs[space_count:]
    me = lax.axis_index("snap")
    _, part_rows, width = firsts[0].shape
    band = out_refs[0].shape[1] // width
    chip_count = len(out_refs) + 1
    near_refs = dict(zip([offset for offset in range(chip_count) if offset != chip_count // 2], out_refs))
    slot = 0
    for offset, out_ref in near_refs.items():
        for k in range(band):
            near = tile_kind(me // 2, me % 2, offset, k, lax.axis_size("snap"))[0]
            lanes = slice(k * width, (k + 1) * width)

            @pl.when(jnp.logical_not(near))
            def _(out_ref=out_ref, lanes=lanes):
                out_ref[0:part_rows, lanes] = jnp.zeros((part_rows, width), jnp.float32)

            @pl.when(near)
            def _(out_ref=out_ref, lanes=lanes, slot=slot):
                out_ref[0:part_rows, lanes] = functools.reduce(jnp.add, [ref[slot] for ref in firsts])

            slot = slot + jnp.where(near, 1, 0)
        put_means(mean_ref, out_ref, part_rows)


def put_means(mean_ref, out_ref, first_row):
    across = out_ref.shape[1] // LANES
    for n in range(mean_ref.shape[0]):
        lanes = slice((n % across) * LANES, (n % across + 1) * LANES)
        out_ref[first_row + n // across : first_row + n // across + 1, lanes] = mean_ref[n : n + 1, :]


def joined_far_kernel(rounds, space_count, *refs):
    seconds, out_refs = refs[:space_count], refs[space_count:]
    me = lax.axis_index("snap")
    chip = me // 2
    _, _, width = seconds[0].shape
    chip_count = lax.axis_size("snap") // 2
    band = chip_count + 1
    slot = 0
    for offset in range(chip_count):
        here = [(0, chip_count)] if offset == 0 else []
        here += [(n + 1, source) for n, (pairs, _) in enumerate(rounds) for source in pairs if pairs[source] == source ^ offset]
        place = 0
        for k in range(band):
            far = tile_kind(chip, me % 2, offset, k, 2 * chip_count)[1]
            for n, source in here:
                mine = far if source == chip_count else jnp.logical_and(far, chip == source)

                @pl.when(mine)
                def _(n=n, slot=slot, place=place):
                    total = functools.reduce(jnp.add, [ref[slot] for ref in seconds])
                    lanes = pl.ds(pl.multiple_of(place * width, width), width)
                    out_refs[n][:, lanes] = total

            slot = slot + jnp.where(far, 1, 0)
            place = place + jnp.where(far, 1, 0)


def collected_kernel(first_chip, rounds, scale, *refs):
    me = lax.axis_index("snap")
    chip, core = me // 2, me % 2
    chip_count = lax.axis_size("snap") // 2
    hub_chips = chip_count // 2
    late = chip_count // 2
    nears, fars, (gram_ref, mean_ref) = refs[: chip_count - 1], refs[chip_count - 1 : -2], refs[-2:]
    nears = dict(zip([offset for offset in range(chip_count) if offset != late], nears))
    part_rows, columns = gram_ref.shape
    is_hub = (chip >= first_chip) & (chip < first_chip + hub_chips)
    total = jnp.zeros((part_rows, columns), jnp.float32)
    for offset, ref in nears.items():
        hub = (chip ^ offset) - first_chip
        held = True if offset < 2 else (hub >= 0) & (hub < hub_chips)
        total = total + jnp.where(held, ref[0:part_rows, :], 0.0)
    gram_ref[...] = total * scale
    for n, ref in enumerate(fars):
        source = jnp.where(is_hub, chip, -1)
        if n:
            source = -1
            for a, b in rounds[n - 1][0].items():
                source = jnp.where(chip == b, a, source)
        place = 0
        for k in range(columns // LANES):
            far = jnp.logical_and(source >= 0, tile_kind(source, core, source ^ chip, k, 2 * chip_count)[1])
            lanes = slice(k * LANES, (k + 1) * LANES)

            @pl.when(far)
            def _(ref=ref, lanes=lanes, place=place):
                sent = ref[:, pl.ds(pl.multiple_of(place * LANES, LANES), LANES)]
                gram_ref[:, lanes] = gram_ref[:, lanes] + sent * scale

            place = place + jnp.where(far, 1, 0)
    mean_rows = mean_ref.shape[0] // hub_chips
    across = columns // LANES
    for offset, ref in nears.items():
        hub = (chip ^ offset) - first_chip
        if offset == 0:
            hub = jnp.where(is_hub, hub, (chip ^ late) - first_chip)

        @pl.when((hub >= 0) & (hub < hub_chips))
        def _(ref=ref, hub=hub):
            for n in range(mean_rows):
                row, lanes = part_rows + n // across, slice((n % across) * LANES, (n % across + 1) * LANES)
                mean_ref[pl.ds(hub * mean_rows + n, 1), :] = ref[row : row + 1, lanes]


def per_device(snapshots):
    snap_count = lax.axis_size("snap")
    space_count = lax.axis_size("space")
    row_count, width = snapshots.shape
    chip_count = snap_count // 2
    first_chip, hub_chips = chip_count // 4, chip_count // 2
    hubs = list(range(2 * first_chip, 2 * (first_chip + hub_chips)))
    rows = row_count // hub_chips
    band = chip_count + 1
    part_rows = width // space_count
    late = chip_count // 2
    early = [offset for offset in range(chip_count) if offset not in (late, late ^ 1)] + [late ^ 1]
    near = 2 * len(early)
    vmem = pl.BlockSpec(memory_space=pltpu.VMEM)

    def shaped(dtype, *shape):
        return jax.ShapeDtypeStruct(shape, dtype)

    def kernel(body, operands, out_shapes, scratch=(), flops=1000, raw=False):
        sizes = [int(np.prod(s.shape)) * jnp.dtype(s.dtype).itemsize for s in (*operands, *out_shapes)]
        sizes += [int(np.prod(s.shape)) * jnp.dtype(s.dtype).itemsize for s in scratch if hasattr(s, "shape") and s.memory_space == pltpu.VMEM]
        return pl.pallas_call(
            body,
            out_shape=list(out_shapes),
            in_specs=[pl.BlockSpec(memory_space=pltpu.HBM) if raw else vmem] * len(operands),
            out_specs=[vmem] * len(out_shapes),
            scratch_shapes=list(scratch),
            cost_estimate=pl.CostEstimate(flops=flops, bytes_accessed=0, transcendentals=0),
            compiler_params=pltpu.CompilerParams(vmem_limit_bytes=sum(sizes) + (6 << 20)),
        )(*operands)

    def hub_of(device):
        chip = device // 2
        is_hub = (chip >= first_chip) & (chip < first_chip + hub_chips)
        return (jnp.where(is_hub, chip, chip ^ late) - first_chip) * rows

    def to_hubs(x, offset, name):
        pairs = [(h ^ (2 * offset), h) for h in hubs]
        if name == "sums" or offset == 1:
            pairs = [(i ^ (2 * offset), i) for i in range(snap_count)]
        elif offset != late:
            pairs = completed(pairs, snap_count)
        return lax.ppermute(x, "snap", pairs)

    def to_other_core(x):
        return lax.ppermute(x, "snap", [(i, i ^ 1) for i in range(snap_count)])

    piece = shaped(snapshots.dtype, rows, width)
    sums = shaped(jnp.float32, rows // LANES, LANES)
    offsets = early + [late]
    own_piece, next_piece = kernel(
        functools.partial(split_kernel, hub_of),
        [pltpu.with_memory_space_constraint(snapshots, pltpu.HBM)],
        [piece] * 2,
        [pltpu.SemaphoreType.DMA((2,))],
        raw=True,
    )
    pieces = {}
    for offset in offsets:
        if offset in (0, 1, late, late ^ 1):
            pieces[offset] = own_piece if offset in (0, late) else next_piece
        elif offset ^ late in pieces:
            pieces[offset] = pieces[offset ^ late]
        else:
            pieces[offset] = lax.dynamic_slice_in_dim(snapshots, hub_of(lax.axis_index("snap") ^ (2 * offset)), rows, 0)
    blocks = {0: own_piece} | {offset: to_hubs(pieces[offset], offset, "bulk") for offset in offsets[1:]}

    distinct = list({id(x): x for x in pieces.values()}.values())
    place = {offset: [x is pieces[offset] for x in distinct].index(True) for offset in offsets}
    (row_sums,) = kernel(sums_kernel, distinct, [shaped(jnp.float32, len(distinct) * (rows // LANES), LANES)])
    chip_sums = kernel(chip_sums_kernel, [row_sums, to_other_core(row_sums)], [sums] * len(distinct))
    came = [chip_sums[place[0]]] + [to_hubs(chip_sums[place[offset]], offset, "sums") for offset in offsets[1:]]
    passed = {offset: to_other_core(blocks[offset]) for offset in offsets}

    first_slots, second_slots = slot_count(snap_count, False), slot_count(snap_count, True)
    half, kept = len(early), len(early) - 1
    products = shaped(jnp.float32, half * width, (near - 1) * width)
    turned, mean_rows, spread, near_held = kernel(
        functools.partial(near_kernel, width * snap_count, half, math.gcd(rows // LANES, CHUNKS)),
        came + [blocks[offset] for offset in early] + [passed[offset] for offset in early if offset != 1],
        [shaped(jnp.bfloat16, (near - 2) * width, rows), sums, shaped(jnp.float32, rows, LANES), products],
        [pltpu.VMEM((rows, (near - 1) * width), jnp.bfloat16)],
        flops=near * near * width * width * rows,
    )
    last_turned, *first = kernel(
        functools.partial(near_last_kernel, half),
        [spread, passed[1], turned, near_held],
        [shaped(jnp.bfloat16, width, rows)] + [shaped(jnp.float32, first_slots, part_rows, width)] * space_count,
        [pltpu.VMEM((rows, width), jnp.bfloat16), pltpu.VMEM((half * width, width), jnp.float32)],
        flops=2 * half * width * width * rows,
    )
    flops = 2 * snap_count * width * width * rows
    (held,) = kernel(
        functools.partial(far_same_kernel, half),
        [spread, blocks[late], turned, last_turned],
        [shaped(jnp.float32, 3 * kept, width, width)],
        [pltpu.VMEM((rows, width), jnp.bfloat16)],
        flops=flops,
    )
    second = kernel(
        functools.partial(far_other_kernel, half),
        [spread, passed[late], turned, held],
        [shaped(jnp.float32, second_slots, part_rows, width)] * space_count,
        [pltpu.VMEM((rows, width), jnp.bfloat16), pltpu.VMEM((kept, width, width), jnp.float32)],
        flops=flops,
    )

    def over_space(parts):
        got = [parts[0]]
        for n in range(1, space_count):
            got.append(lax.ppermute(parts[n], "space", [(s, s ^ n) for s in range(space_count)]))
        return got

    mean_space = -(-(-(-(rows // LANES) // band)) // 8) * 8
    slab = shaped(jnp.float32, part_rows + mean_space, band * width)
    near_slabs = kernel(
        functools.partial(joined_near_kernel, space_count), [mean_rows, *over_space(first)], [slab] * len(early)
    )

    nears = [near_slabs[0]]
    for offset, x in zip(early[1:], near_slabs[1:]):
        sources = range(snap_count) if offset == 1 else hubs
        pairs = completed([(i, i ^ (2 * offset)) for i in sources], snap_count)
        nears.append(lax.ppermute(x, "snap", pairs))
    rounds = far_rounds(chip_count)
    far_slabs = kernel(
        functools.partial(joined_far_kernel, rounds, space_count),
        over_space(second),
        [shaped(jnp.float32, part_rows, count * width) for count in [band] + [count for _, count in rounds]],
    )
    fars = [far_slabs[0]]
    for n, (pairs, _) in enumerate(rounds):
        devices = [(2 * a + core, 2 * b + core) for a, b in pairs.items() for core in (0, 1)]
        fars.append(lax.ppermute(far_slabs[n + 1], "snap", completed(devices, snap_count)))
    gram_band, mean_field = kernel(
        functools.partial(collected_kernel, first_chip, rounds, 1.0 / (row_count * space_count)),
        nears + fars,
        [shaped(jnp.float32, part_rows, band * width), shaped(jnp.float32, row_count // LANES, LANES)],
    )
    return gram_band, mean_field.reshape(row_count)


def solution(mesh):
    return jax.shard_map(
        per_device,
        mesh=mesh,
        in_specs=(P("space", "snap"),),
        out_specs=(P(("snap", "space"), None), P("space")),
        check_vma=False,
    )
```
